128 devices in a mesh: front: 8 (over z_hi, x), row: 8 (over y, core), col: 2 (over z_lo).
Axes of the slice: x: 4, y: 4, z: 4 (z_hi: 2, z_lo: 2; z = z_hi * 2 + z_lo), core: 2. Of those that a mesh axis runs over, the one named last changes fastest.
Arguments:
- pivot_block: float32 [16, 512, 512], P(('front', 'col'), 'row'), as said below
- panel_rows: float32 [16, 4096, 512], P(('front', 'col'), 'row'), may hold values from -0.875 to 0.875
- update_block: float32 [16, 4096, 4096], P(('front', 'col'), 'row'), as said below
- tile_map: int32 [16, 32], replicated, may hold values from 0 to 95, as said below
Outputs:
- pivot_factor: float32 [16, 512, 512], P(('front', 'col'), 'row')
- panel_factor: float32 [16, 4096, 512], P(('front', 'col'), 'row')
- parent_update: float32 [2, 12288, 12288], P('col', 'front', 'row')
The draws below stay inside these ranges and needn't reach their ends.
Inputs may be any that keep to these rules, and one draw needn't show every extreme that they name: `pivot_block`: each child's pivot block is symmetric positive definite. `update_block`: each child's update block is symmetric. `tile_map`: row c lists, strictly increasing, the parent tiles that receive child c's 32 tiles; child c belongs to parent c % 2. At most 5 entries of one row fall in any aligned block of 12 parent tiles, and exactly 5 do in some block.
All inputs are finite; a program needn't handle non-finite values.
Results may differ from the reference program's by a relative error of at most 0.0001.
Values sent between devices are 32-bit elements; how exact they have to be, the bound alone decides.
No kernel may reach another device: no remote copies, remote signals or barrier semaphores. Data moves between devices by JAX's collectives and lax.ppermute only.
A program may use at most 192 MiB of HBM per device.

```python
import math
import jax
import jax.numpy as jnp
from jax import lax

PANEL = 512
TILE = 128
CONTRIB = 4096
PARENT = 12288
CHILDREN = 16
CTILES = 32
PTILES = 96
BLOCK = 12
N_COL = 2


def draw_pivot_block(key, part):

    def draw_child(subkey):
        key_jitter, key_diagonal = jax.random.split(subkey)
        spread_max = 1.8 / PANEL
        jitter = jax.random.uniform(key_jitter, (PANEL, PANEL), jnp.float32, -spread_max, spread_max)
        symmetric = 0.5 * (jitter + jitter.T)
        diagonal = jnp.exp(jax.random.uniform(key_diagonal, (PANEL,), jnp.float32, math.log(2.0), math.log(8.0)))
        identity = jnp.eye(PANEL, dtype=jnp.float32)
        return symmetric * (1.0 - identity) + identity * diagonal[None, :]
    return jax.vmap(draw_child)(jax.random.split(key, CHILDREN))


def draw_update_block(key, part):

    def draw_child(subkey):
        values = jax.random.normal(subkey, (CONTRIB, CONTRIB), jnp.float32)
        return 0.7071 * (values + values.T)
    return jax.vmap(draw_child)(jax.random.split(key, CHILDREN))


def draw_tile_map(key, part):
    blocks = PTILES // BLOCK
    base_count = CTILES // blocks
    key_hot, key_children = jax.random.split(key)
    hot_blocks = jax.random.randint(key_hot, (N_COL,), 0, blocks)

    def draw_child(subkey, child_index):
        key_partner, key_order, key_flip, key_within = jax.random.split(subkey, 4)
        hot_block = hot_blocks[child_index % N_COL]
        partner = (hot_block + 1 + jax.random.randint(key_partner, (), 0, blocks - 1)) % blocks
        block_ids = jnp.arange(blocks, dtype=jnp.int32)
        ranking = jax.random.permutation(key_order, blocks).astype(jnp.int32)
        pinned = ((block_ids == hot_block) | (block_ids == partner)).astype(jnp.int32)
        ordering = jnp.argsort(ranking + blocks * pinned)
        position = jnp.argsort(ordering).astype(jnp.int32)
        pair_total = (blocks - 2) // 2
        coin_flip = jax.random.randint(key_flip, (blocks,), 0, 2)
        in_pair = (position < 2 * pair_total) & (pinned == 0)
        parity = 1 - 2 * (position % 2)
        change = jnp.where(in_pair, parity * coin_flip[position // 2], 0)
        change = change + (block_ids == hot_block).astype(jnp.int32) - (block_ids == partner).astype(jnp.int32)
        counts = base_count + change
        within_rank = jax.vmap(lambda inner: jax.random.permutation(inner, BLOCK))(jax.random.split(key_within, blocks))
        chosen = (within_rank < counts[:, None]).reshape(-1)
        tile_ids = jnp.arange(PTILES, dtype=jnp.int32)
        return jnp.argsort(jnp.where(chosen, tile_ids, tile_ids + PTILES))[:CTILES].astype(jnp.int32)
    return jax.vmap(draw_child)(jax.random.split(key_children, CHILDREN), jnp.arange(CHILDREN, dtype=jnp.int32))


def level_of(key, dims, cuts, least, high):
    def one(dim, shards_of):
        heights = jax.random.uniform(jax.random.fold_in(jax.random.fold_in(key, 6), dim), (shards_of,), jnp.float32, least / len(cuts), high / len(cuts))
        return jnp.repeat(jnp.exp(heights), dims[dim] // shards_of).reshape((-1,) + (1,) * (len(dims) - dim - 1))

    level = one(*cuts[0])
    for cut in cuts[1:]:
        level = level * one(*cut)
    return level


def centred(stream_key, extent, width, reach, shards=(), held_as=jnp.bfloat16):
    gain = level_of(stream_key, extent, shards, -0.22, 0.18) if shards else 1.0
    entries = jax.random.normal(stream_key, extent, jnp.float32) * width * gain
    return jnp.minimum(jnp.maximum(entries, -reach), reach).astype(held_as)


def setup_inputs(seed: int = 0) -> dict:
    splits = jax.random.split(jax.random.key(seed), 5)
    pivot_block = draw_pivot_block(jax.random.fold_in(splits[4], 71), 0)
    panel_rows = centred(splits[1], (CHILDREN, CONTRIB, PANEL), 0.15, 0.875, ((0, 16), (1, 8)), jnp.float32)
    update_block = draw_update_block(jax.random.fold_in(splits[4], 71), 0)
    tile_map = draw_tile_map(jax.random.fold_in(splits[4], 71), 0)
    return dict(pivot_block=pivot_block, panel_rows=panel_rows, update_block=update_block, tile_map=tile_map)


def solve_panel(lower_factor, panel_block):
    return jax.scipy.linalg.solve_triangular(lower_factor, panel_block.T, lower=True).T

def reference(pivot_block, panel_rows, update_block, tile_map):
    lower_factor = jnp.linalg.cholesky(pivot_block)
    panel_factor = jax.vmap(solve_panel)(lower_factor, panel_rows)
    offsets = jnp.arange(TILE, dtype=jnp.int32)

    def add_child(child_index, parents):
        factor = lax.dynamic_index_in_dim(panel_factor, child_index, 0, keepdims=False)
        update = lax.dynamic_index_in_dim(update_block, child_index, 0, keepdims=False)
        contribution = update - jnp.dot(factor, factor.T, precision=lax.Precision.HIGHEST)
        tile_ids = lax.dynamic_index_in_dim(tile_map, child_index, 0, keepdims=False)
        positions = (tile_ids[:, None] * TILE + offsets[None, :]).reshape(-1).astype(jnp.int32)
        return parents.at[child_index % N_COL, positions[:, None], positions[None, :]].add(contribution)
    parents = lax.fori_loop(0, CHILDREN, add_child, jnp.zeros((N_COL, PARENT, PARENT), jnp.float32))
    return (lower_factor, panel_factor, parents)
```

```python
import jax
import jax.numpy as jnp
from jax import lax
from jax.experimental import pallas as pl
from jax.experimental.pallas import tpu as pltpu
from jax.sharding import PartitionSpec as P

TILE = 128
BLOCK = 12
SLOTS = 5
GROUPS = 8
CTILES = 32
WIN = SLOTS * TILE
SIDE = BLOCK * TILE
CHUNKS = ((0, 1), (1, 2), (3, 2))
HI = lax.Precision.HIGHEST
F32 = jnp.float32


def any_spec():
    return pl.BlockSpec(memory_space=pl.ANY)


def smem_spec():
    return pl.BlockSpec(memory_space=pltpu.SMEM)


def vmem_spec():
    return pl.BlockSpec(memory_space=pltpu.VMEM)


def window_starts(tile_ids):
    owners = tile_ids // BLOCK
    blocks = jnp.arange(GROUPS, dtype=jnp.int32)
    starts = jnp.sum((owners[..., None, :] < blocks[:, None]).astype(jnp.int32), axis=-1)
    return jnp.minimum(starts, CTILES - SLOTS)


def slot_targets(child_maps, block_me):
    first = jnp.sum((child_maps // BLOCK < block_me).astype(jnp.int32), axis=1)
    first = jnp.minimum(first, CTILES - SLOTS)
    picks = first[:, None] + jnp.arange(SLOTS, dtype=jnp.int32)[None, :]
    tiles = jnp.take_along_axis(child_maps, picks, axis=1)
    return jnp.where(tiles // BLOCK == block_me, tiles - block_me * BLOCK, -1)


def factor_kernel(k, *refs):
    a_ref = refs[0]
    work_ref, urow_ref, w_ref, uw = refs[-4:]
    order = a_ref.shape[0]
    sub = lax.broadcasted_iota(jnp.int32, (8, TILE), 0)
    lane = lax.broadcasted_iota(jnp.int32, (8, TILE), 1)
    c0 = k * TILE
    c1 = c0 + TILE
    uw[...] = jnp.zeros_like(uw)

    def panel(p, carry):
        r0 = pl.multiple_of(p * 8, 8)
        shift = (TILE - r0) % TILE
        rows = a_ref[pl.ds(c0 + r0, 8), c0:c1]
        eye = (lane == r0 + sub).astype(F32)
        lhs = pltpu.roll(uw[:, 0:TILE], shift, 1)[:, 0:8]
        upd = lax.dot_general(lhs, uw[...], (((0,), (0,)), ((), ())), precision=HI, preferred_element_type=F32)
        ru = rows - upd[:, 0:TILE]
        rw = eye - upd[:, TILE:]
        diag = pltpu.roll(ru, shift, 1)
        cols = [jnp.broadcast_to(diag[:, j : j + 1], (8, TILE)) for j in range(8)]
        pivots = jnp.zeros((8, TILE), F32)
        for j in range(8):
            d = jnp.broadcast_to(cols[j][j : j + 1, :], (8, TILE))
            pivots = jnp.where(sub == j, d, pivots)
            f = jnp.where(sub > j, cols[j] / d, 0.0)
            ru = ru - f * jnp.broadcast_to(ru[j : j + 1, :], (8, TILE))
            rw = rw - f * jnp.broadcast_to(rw[j : j + 1, :], (8, TILE))
            for m in range(j + 1, 8):
                cols[m] = cols[m] - f * jnp.broadcast_to(cols[m][j : j + 1, :], (8, TILE))
        scale = lax.rsqrt(pivots)
        uw[pl.ds(r0, 8), 0:TILE] = jnp.where(lane >= r0 + sub, ru * scale, 0.0)
        uw[pl.ds(r0, 8), TILE:] = rw * scale
        return carry

    lax.fori_loop(0, TILE // 8, panel, 0)
    w = uw[:, TILE:]
    w_ref[...] = w
    if k:
        urow_ref[:, 0:c0] = jnp.zeros((TILE, c0), F32)
    urow_ref[:, c0:c1] = uw[:, 0:TILE]
    if c1 < order:
        urow = jnp.dot(w, a_ref[c0:c1, c1:], precision=HI, preferred_element_type=F32)
        urow_ref[:, c1:] = urow
        work_ref[c1:, c1:] = a_ref[c1:, c1:] - lax.dot_general(
            urow, urow, (((0,), (0,)), ((), ())), precision=HI, preferred_element_type=F32
        )


def factor_step(k, work, after):
    order = work.shape[0]
    return pl.pallas_call(
        lambda *refs: factor_kernel(k, *refs),
        out_shape=(
            jax.ShapeDtypeStruct((order, order), F32),
            jax.ShapeDtypeStruct((TILE, order), F32),
            jax.ShapeDtypeStruct((TILE, TILE), F32),
        ),
        in_specs=[vmem_spec()] + [any_spec()] * len(after),
        out_specs=(vmem_spec(), vmem_spec(), vmem_spec()),
        scratch_shapes=[pltpu.VMEM((TILE, 2 * TILE), F32)],
        input_output_aliases={0: 0},
        cost_estimate=pl.CostEstimate(flops=5_000_000_000, transcendentals=0, bytes_accessed=4_000_000),
        name="factor",
    )(work, *after)


def solve_rows(x_ref, u_refs, w_refs):
    for k in range(len(w_refs)):
        c0 = k * TILE
        c1 = c0 + TILE
        rhs = x_ref[:, c0:c1]
        if k:
            above = jnp.concatenate([u_refs[j][:, c0:c1] for j in range(k)], axis=0)
            rhs = rhs - jnp.dot(x_ref[:, 0:c0], above, precision=HI, preferred_element_type=F32)
        x_ref[:, c0:c1] = lax.dot_general(
            rhs, w_refs[k][...], (((1,), (1,)), ((), ())), precision=HI, preferred_element_type=F32
        )


def solve_kernel(start_ref, *refs):
    steps = (len(refs) - 9) // 2
    u_refs, w_refs = refs[:steps], refs[steps : 2 * steps]
    pieces = refs[2 * steps : 2 * steps + 5]
    own_ref, win_ref, band, sems = refs[2 * steps + 5 :]
    far_low, low, own = pieces[:3]
    copies = []
    at = 0
    for n, piece in enumerate(pieces):
        rows = piece.shape[0]
        copies.append(pltpu.make_async_copy(piece, band.at[pl.ds(at, rows)], sems.at[n]))
        at += rows
    for copy in copies:
        copy.start()
    for copy in copies:
        copy.wait()
    start = pl.multiple_of(start_ref[0] * TILE, TILE)
    own_at = far_low.shape[0] + low.shape[0]
    win_ref[...] = band[pl.ds(start, WIN), :]
    own_ref[...] = band[own_at : own_at + own.shape[0], :]
    solve_rows(win_ref, u_refs, w_refs)
    solve_rows(own_ref, u_refs, w_refs)


def solve(start, urows, inverses, pieces):
    rows = sum(piece.shape[0] for piece in pieces)
    width = urows[0].shape[1]
    own = pieces[2].shape
    return pl.pallas_call(
        solve_kernel,
        out_shape=(jax.ShapeDtypeStruct(own, F32), jax.ShapeDtypeStruct((WIN, width), F32)),
        in_specs=[smem_spec()] + [vmem_spec()] * (2 * len(urows)) + [any_spec()] * 5,
        out_specs=(vmem_spec(), vmem_spec()),
        scratch_shapes=[pltpu.VMEM((rows, width), F32), pltpu.SemaphoreType.DMA((5,))],
        compiler_params=pltpu.CompilerParams(vmem_limit_bytes=40 * 1024 * 1024),
        cost_estimate=pl.CostEstimate(flops=6_000_000_000, transcendentals=0, bytes_accessed=12_000_000),
        name="solve",
    )(start, *urows, *inverses, *pieces)


def pack_columns_kernel(starts_ref, u_ref, *rest):
    outs, sems = rest[:-1], rest[-1]
    copies = []
    for c, (slot, width) in enumerate(CHUNKS):
        for k in range(GROUPS):
            n = c * GROUPS + k
            at = pl.multiple_of((starts_ref[k] + slot) * TILE, TILE)
            copies.append(pltpu.make_async_copy(u_ref.at[:, pl.ds(at, width * TILE)], outs[n], sems.at[n]))
    for copy in copies:
        copy.start()
    for copy in copies:
        copy.wait()


def pack_columns(turned_starts, update):
    rows = update.shape[0]
    shapes = [jax.ShapeDtypeStruct((rows, width * TILE), F32) for _, width in CHUNKS for _ in range(GROUPS)]
    outs = pl.pallas_call(
        pack_columns_kernel,
        out_shape=tuple(shapes),
        in_specs=[smem_spec(), any_spec()],
        out_specs=tuple(any_spec() for _ in shapes),
        scratch_shapes=[pltpu.SemaphoreType.DMA((len(shapes),))],
        cost_estimate=pl.CostEstimate(flops=0, transcendentals=0, bytes_accessed=20_000_000),
        name="pack_columns",
    )(turned_starts, update)
    return [outs[c * GROUPS : (c + 1) * GROUPS] for c in range(len(CHUNKS))]


def pack_rows_kernel(group_ref, slot_ref, *rest):
    pieces, out_ref, sems = rest[:GROUPS], rest[GROUPS], rest[GROUPS + 1]
    copies = []
    for k in range(GROUPS):
        for q in range(CTILES // GROUPS):
            n = k * (CTILES // GROUPS) + q
            src = pieces[k].at[pl.ds(q * TILE, TILE)]
            copies.append(pltpu.make_async_copy(src, out_ref.at[group_ref[n], slot_ref[n]], sems.at[n]))
    for copy in copies:
        copy.start()
    for copy in copies:
        copy.wait()


def pack_rows(groups, slots, pieces):
    width = pieces[0].shape[1]
    return pl.pallas_call(
        pack_rows_kernel,
        out_shape=jax.ShapeDtypeStruct((GROUPS, SLOTS, TILE, width), F32),
        in_specs=[smem_spec(), smem_spec()] + [any_spec()] * GROUPS,
        out_specs=any_spec(),
        scratch_shapes=[pltpu.SemaphoreType.DMA((CTILES,))],
        cost_estimate=pl.CostEstimate(flops=0, transcendentals=0, bytes_accessed=5_000_000),
        name="pack_rows",
    )(groups, slots, *pieces)


def split(x):
    high = x.astype(jnp.bfloat16)
    return high, (x - high.astype(F32)).astype(jnp.bfloat16)


def assemble_kernel(rows_ref, cols_ref, *rest):
    parts = rest[: len(CHUNKS)]
    xf_ref, xr_ref, out_ref, acc, sem = rest[len(CHUNKS) :]
    child = pl.program_id(0)

    @pl.when(child == 0)
    def _():
        acc[...] = jnp.zeros_like(acc)

    rh, rl = split(xr_ref[0])
    rhs = jnp.concatenate([rh, rl, rh], axis=1)
    for s in range(SLOTS):
        row = rows_ref[child, s]

        @pl.when(row >= 0)
        def _():
            fh, fl = split(xf_ref[0, s * TILE : (s + 1) * TILE, :])
            lhs = jnp.concatenate([fh, fh, fl], axis=1)
            prod = lax.dot_general(lhs, rhs, (((1,), (1,)), ((), ())), preferred_element_type=F32)
            at = pl.multiple_of(row * TILE, TILE)
            for c, (slot, width) in enumerate(CHUNKS):
                for w in range(width):
                    t = slot + w
                    col = cols_ref[child, t]

                    @pl.when(col >= 0)
                    def _():
                        tile = parts[c][0, s * TILE : (s + 1) * TILE, w * TILE : (w + 1) * TILE]
                        acc[col, pl.ds(at, TILE), :] += tile - prod[:, t * TILE : (t + 1) * TILE]

    @pl.when(child == pl.num_programs(0) - 1)
    def _():
        copies = [
            pltpu.make_async_copy(acc.at[b], out_ref.at[:, pl.ds(b * TILE, TILE)], sem.at[b]) for b in range(BLOCK)
        ]
        for copy in copies:
            copy.start()
        for copy in copies:
            copy.wait()


def assemble(rows, cols, parts, xf, xr):
    width = xf.shape[2]
    block = lambda n: pl.BlockSpec((1, WIN, n), lambda c: (c, 0, 0))
    return pl.pallas_call(
        assemble_kernel,
        grid=(GROUPS,),
        out_shape=jax.ShapeDtypeStruct((SIDE, SIDE), F32),
        in_specs=[smem_spec(), smem_spec()] + [block(w * TILE) for _, w in CHUNKS] + [block(width)] * 2,
        out_specs=any_spec(),
        scratch_shapes=[pltpu.VMEM((BLOCK, SIDE, TILE), F32), pltpu.SemaphoreType.DMA((BLOCK,))],
        compiler_params=pltpu.CompilerParams(vmem_limit_bytes=48 * 1024 * 1024),
        cost_estimate=pl.CostEstimate(flops=20_000_000_000, transcendentals=0, bytes_accessed=40_000_000),
        name="assemble",
    )(rows, cols, *parts, xf, xr)


def local(pivot_block, panel_rows, update_block, tile_map):
    row_me = lax.axis_index("row")
    front_me = lax.axis_index("front")
    col_me = lax.axis_index("col")
    share = pivot_block.shape[1]
    slab = panel_rows[0]
    half = slab.shape[0] // 2

    tile_ids = lax.dynamic_index_in_dim(tile_map, front_me * 2 + col_me, 0, keepdims=False)
    starts = window_starts(tile_ids)
    child_maps = jnp.take(tile_map, jnp.arange(GROUPS, dtype=jnp.int32) * 2 + col_me, axis=0)
    row_slots = slot_targets(child_maps, front_me)
    col_slots = slot_targets(child_maps, row_me)

    pivot = lax.all_gather(pivot_block[0], "row", axis=0, tiled=True)

    up = lambda n: [(i, i + n) for i in range(GROUPS - n)]
    down = lambda n: [(i + n, i) for i in range(GROUPS - n)]
    pieces = (
        lax.ppermute(slab[half:], "row", up(2)),
        lax.ppermute(slab, "row", up(1)),
        slab,
        lax.ppermute(slab, "row", down(1)),
        lax.ppermute(slab[:half], "row", down(2)),
    )
    start = lax.dynamic_index_in_dim(starts, row_me, 0, keepdims=True) - 4 * row_me + 6

    groups = tile_ids // BLOCK
    order = (row_me - jnp.arange(GROUPS, dtype=jnp.int32)) % GROUPS
    tiles = (order[:, None] * 4 + jnp.arange(4, dtype=jnp.int32)[None, :]).reshape(-1)
    tile_groups = jnp.take(groups, tiles)
    tile_slots = tiles - jnp.take(starts, tile_groups)
    ahead = jnp.take(starts, (row_me + jnp.arange(GROUPS, dtype=jnp.int32)) % GROUPS)

    ring = lambda k: [(i, (i + k) % GROUPS) for i in range(GROUPS)]
    chunks = pack_columns(ahead, update_block[0])
    parts = []
    marks = [chunks[0][0]]
    for packed in chunks:
        arrived = [packed[0]] + [lax.ppermute(packed[k], "row", ring(k)) for k in range(1, GROUPS)]
        arrived = pack_rows(tile_groups, tile_slots, arrived).reshape(GROUPS, WIN, -1)
        marks.append(arrived)
        parts.append(lax.all_to_all(arrived, "front", split_axis=0, concat_axis=0, tiled=True))

    urows, inverses = [], []
    work = pivot
    for k in range(4):
        work, urow, inverse = factor_step(k, work, marks[k : k + 1] if k < 3 else [])
        urows.append(urow)
        inverses.append(inverse)
    own_factor, window = solve(start, urows, inverses, pieces)

    mirror = [(a * GROUPS + b, b * GROUPS + a) for a in range(GROUPS) for b in range(GROUPS)]
    turned = lax.ppermute(window, ("front", "row"), mirror)
    xf = lax.all_gather(turned, "row", axis=0)
    xr = lax.all_gather(window, "front", axis=0)
    parent = assemble(row_slots, col_slots, parts, xf, xr)
    lower_rows = jnp.concatenate([lax.dynamic_slice_in_dim(urow, row_me * share, share, 1) for urow in urows], axis=0).T
    return (lower_rows[None], own_factor[None], parent[None])


def solution(mesh):
    return jax.shard_map(
        local,
        mesh=mesh,
        in_specs=(
            P(("front", "col"), "row", None),
            P(("front", "col"), "row", None),
            P(("front", "col"), "row", None),
            P(),
        ),
        out_specs=(
            P(("front", "col"), "row", None),
            P(("front", "col"), "row", None),
            P("col", "front", "row"),
        ),
        check_vma=False,
    )
```

```python
import jax
import jax.numpy as jnp
from jax import lax
from jax.experimental import pallas as pl
from jax.experimental.pallas import tpu as pltpu
from jax.sharding import PartitionSpec as P

TILE = 128
BLOCK = 12
SLOTS = 5
GROUPS = 8
CTILES = 32
WIN = SLOTS * TILE
SIDE = BLOCK * TILE
CHUNKS = ((0, 1), (1, 2), (3, 2))
HI = lax.Precision.HIGHEST
F32 = jnp.float32


def any_spec():
    return pl.BlockSpec(memory_space=pl.ANY)


def hbm(x):
    return pltpu.with_memory_space_constraint(x, pltpu.HBM)


def smem_spec():
    return pl.BlockSpec(memory_space=pltpu.SMEM)


def vmem_spec():
    return pl.BlockSpec(memory_space=pltpu.VMEM)


def window_starts(tile_ids):
    owners = tile_ids // BLOCK
    blocks = jnp.arange(GROUPS, dtype=jnp.int32)
    starts = jnp.sum((owners[..., None, :] < blocks[:, None]).astype(jnp.int32), axis=-1)
    return jnp.minimum(starts, CTILES - SLOTS)


def slot_targets(child_maps, block_me):
    first = jnp.sum((child_maps // BLOCK < block_me).astype(jnp.int32), axis=1)
    first = jnp.minimum(first, CTILES - SLOTS)
    picks = first[:, None] + jnp.arange(SLOTS, dtype=jnp.int32)[None, :]
    tiles = jnp.take_along_axis(child_maps, picks, axis=1)
    return jnp.where(tiles // BLOCK == block_me, tiles - block_me * BLOCK, -1)


def factor_kernel(a_ref, *refs):
    u_ref, v_ref, work, uw = refs[-4:]
    order = a_ref.shape[0]
    sub = lax.broadcasted_iota(jnp.int32, (8, TILE), 0)
    lane = lax.broadcasted_iota(jnp.int32, (8, TILE), 1)
    work[...] = a_ref[...]
    u_ref[...] = jnp.zeros_like(u_ref)
    v_ref[...] = jnp.zeros_like(v_ref)
    for k in range(order // TILE):
        c0 = k * TILE
        c1 = c0 + TILE
        uw[...] = jnp.zeros_like(uw)

        def panel(p, carry):
            r0 = pl.multiple_of(p * 8, 8)
            shift = (TILE - r0) % TILE
            rows = work[pl.ds(c0 + r0, 8), c0:c1]
            eye = (lane == r0 + sub).astype(F32)
            lhs = pltpu.roll(uw[:, 0:TILE], shift, 1)[:, 0:8]
            upd = lax.dot_general(lhs, uw[...], (((0,), (0,)), ((), ())), precision=HI, preferred_element_type=F32)
            ru = rows - upd[:, 0:TILE]
            rw = eye - upd[:, TILE:]
            diag = pltpu.roll(ru, shift, 1)
            cols = [jnp.broadcast_to(diag[:, j : j + 1], (8, TILE)) for j in range(8)]
            pivots = jnp.zeros((8, TILE), F32)
            for j in range(8):
                d = jnp.broadcast_to(cols[j][j : j + 1, :], (8, TILE))
                pivots = jnp.where(sub == j, d, pivots)
                f = jnp.where(sub > j, cols[j] / d, 0.0)
                ru = ru - f * jnp.broadcast_to(ru[j : j + 1, :], (8, TILE))
                rw = rw - f * jnp.broadcast_to(rw[j : j + 1, :], (8, TILE))
                for m in range(j + 1, 8):
                    cols[m] = cols[m] - f * jnp.broadcast_to(cols[m][j : j + 1, :], (8, TILE))
            scale = lax.rsqrt(pivots)
            uw[pl.ds(r0, 8), 0:TILE] = jnp.where(lane >= r0 + sub, ru * scale, 0.0)
            uw[pl.ds(r0, 8), TILE:] = rw * scale
            return carry

        lax.fori_loop(0, TILE // 8, panel, 0)
        w = uw[:, TILE:]
        u_ref[c0:c1, c0:c1] = uw[:, 0:TILE]
        if c1 < order:
            urow = jnp.dot(w, work[c0:c1, c1:], precision=HI, preferred_element_type=F32)
            u_ref[c0:c1, c1:] = urow
            work[c1:, c1:] = work[c1:, c1:] - lax.dot_general(
                urow, urow, (((0,), (0,)), ((), ())), precision=HI, preferred_element_type=F32
            )
        wt = w.T
        v_ref[c0:c1, c0:c1] = wt
        if k:
            above = jnp.dot(u_ref[0:c0, c0:c1], wt, precision=HI, preferred_element_type=F32)
            v_ref[0:c0, c0:c1] = -jnp.dot(v_ref[0:c0, 0:c0], above, precision=HI, preferred_element_type=F32)


def factor(pivot, after):
    whole = jax.ShapeDtypeStruct(pivot.shape, F32)
    return pl.pallas_call(
        factor_kernel,
        out_shape=(whole, whole),
        in_specs=[vmem_spec()] + [any_spec()] * len(after),
        out_specs=(vmem_spec(), vmem_spec()),
        scratch_shapes=[pltpu.VMEM(pivot.shape, F32), pltpu.VMEM((TILE, 2 * TILE), F32)],
        compiler_params=pltpu.CompilerParams(vmem_limit_bytes=16 * 1024 * 1024),
        cost_estimate=pl.CostEstimate(flops=20_000_000_000, transcendentals=0, bytes_accessed=4_000_000),
        name="factor",
    )(pivot, *after)


def split(x):
    high = x.astype(jnp.bfloat16)
    return high, (x - high.astype(F32)).astype(jnp.bfloat16)


def solve_kernel(all_ref, own_ref, v_ref, *refs):
    high_ref, low_ref, out_ref, rhs = refs[-4:]
    order = v_ref.shape[0]

    @pl.when(pl.program_id(0) == 0)
    def _():
        vh, vl = split(v_ref[...])
        rhs[0:order] = vh
        rhs[order : 2 * order] = vl
        rhs[2 * order :] = vh
        out_ref[...] = jnp.dot(own_ref[...], v_ref[...], precision=HI, preferred_element_type=F32)

    bh, bl = split(all_ref[...])
    lhs = jnp.concatenate([bh, bh, bl], axis=1)
    x = jnp.dot(lhs, rhs[...], preferred_element_type=F32)
    high_ref[...], low_ref[...] = split(x)


def solve(panel_all, slab, inverse, after):
    rows, order = slab.shape
    blocks = panel_all.shape[0] // rows
    whole = lambda shape: pl.BlockSpec(shape, lambda i: (0, 0))
    block = pl.BlockSpec((rows, order), lambda i: (i, 0))
    return pl.pallas_call(
        solve_kernel,
        grid=(blocks,),
        out_shape=(
            pltpu.HBM(panel_all.shape, jnp.bfloat16),
            pltpu.HBM(panel_all.shape, jnp.bfloat16),
            jax.ShapeDtypeStruct(slab.shape, F32),
        ),
        in_specs=[block, whole(slab.shape), whole(inverse.shape)] + [any_spec()] * len(after),
        out_specs=(block, block, whole(slab.shape)),
        scratch_shapes=[pltpu.VMEM((3 * order, order), jnp.bfloat16)],
        compiler_params=pltpu.CompilerParams(vmem_limit_bytes=32 * 1024 * 1024),
        cost_estimate=pl.CostEstimate(flops=8_000_000_000, transcendentals=0, bytes_accessed=20_000_000),
        name="solve",
    )(hbm(panel_all), slab, inverse, *after)


def pack_columns_kernel(starts_ref, turned_ref, u_ref, first_ref, *rest):
    outs, (held, in_sems, out_sems) = rest[:-3], rest[-3:]
    bands = in_sems.shape[0]
    rows = u_ref.shape[0] // bands
    loads = []
    for b in range(bands):
        band = pl.ds(b * rows, rows)
        loads.append(pltpu.make_async_copy(u_ref.at[band], held.at[band], in_sems.at[b]))
    for load in loads:
        load.start()
    stores = []
    for b in range(bands):
        band = pl.ds(b * rows, rows)
        loads[b].wait()
        for k in range(GROUPS):
            for c, (slot, width) in enumerate(CHUNKS):
                starts = turned_ref if c else starts_ref
                at = pl.multiple_of((starts[k] + slot) * TILE, TILE)
                src = held.at[band, pl.ds(at, width * TILE)]
                dst = outs[(c - 1) * GROUPS + k].at[band] if c else first_ref.at[k, band]
                store = pltpu.make_async_copy(src, dst, out_sems.at[b, c, k])
                store.start()
                stores.append(store)
    for store in stores:
        store.wait()


def pack_columns(starts, turned_starts, update):
    rows = update.shape[0]
    first, *others = (width * TILE for _, width in CHUNKS)
    pieces = tuple(pltpu.HBM((rows, other), F32) for other in others for _ in range(GROUPS))
    outs = pl.pallas_call(
        pack_columns_kernel,
        out_shape=(pltpu.HBM((GROUPS, rows, first), F32), *pieces),
        in_specs=[smem_spec()] * 2 + [any_spec()],
        out_specs=(any_spec(),) * (1 + len(pieces)),
        scratch_shapes=[
            pltpu.VMEM(update.shape, F32),
            pltpu.SemaphoreType.DMA((4,)),
            pltpu.SemaphoreType.DMA((4, len(CHUNKS), GROUPS)),
        ],
        compiler_params=pltpu.CompilerParams(vmem_limit_bytes=20 * 1024 * 1024),
        cost_estimate=pl.CostEstimate(flops=0, transcendentals=0, bytes_accessed=20_000_000),
        name="pack_columns",
    )(starts, turned_starts, hbm(update))
    return outs[0], [outs[1 + n * GROUPS : 1 + (n + 1) * GROUPS] for n in range(len(others))]


def form_kernel(slot, count, group_ref, slot_ref, me_ref, *rest):
    pieces = rest[:count]
    xh_ref, xl_ref = rest[count : count + 2]
    out_ref, held, xh, xl, ph, plow, pick_sems, x_sems, in_sems, out_sems = rest[-10:]
    rows, width = held.shape[1:]
    per = CTILES // GROUPS
    sel = pl.multiple_of((me_ref[1] + slot) * TILE, TILE)

    def slab_of(k):
        return k if count == 1 else (me_ref[0] + GROUPS - k) % GROUPS

    def x_loads(k):
        band = pl.ds(pl.multiple_of(slab_of(k) * rows, rows), rows)
        return [
            pltpu.make_async_copy(src.at[band], dst.at[k], x_sems.at[n, k])
            for n, (src, dst) in enumerate(((xh_ref, xh), (xl_ref, xl)))
        ]

    picks = [
        pltpu.make_async_copy(src.at[pl.ds(sel, width)], dst, pick_sems.at[n])
        for n, (src, dst) in enumerate(((xh_ref, ph), (xl_ref, plow)))
    ]
    for copy in picks:
        copy.start()
    for k in range(GROUPS):
        for copy in x_loads(k):
            copy.start()
        src = pieces[0].at[k] if count == 1 else pieces[k]
        pltpu.make_async_copy(src, held.at[k], in_sems.at[k]).start()
    for copy in picks:
        copy.wait()
    rhs = jnp.concatenate([ph[...], plow[...], ph[...]], axis=1)

    def source(k, carry):
        for copy in x_loads(k):
            copy.wait()
        lhs = jnp.concatenate([xh[k], xh[k], xl[k]], axis=1)
        prod = lax.dot_general(lhs, rhs, (((1,), (1,)), ((), ())), preferred_element_type=F32)
        src = pieces[0].at[0] if count == 1 else pieces[0]
        pltpu.make_async_copy(src, held.at[k], in_sems.at[k]).wait()
        held[k] -= prod
        for q in range(per):
            tile = slab_of(k) * per + q
            src = held.at[k, pl.ds(q * TILE, TILE)]
            pltpu.make_async_copy(src, out_ref.at[group_ref[tile], slot_ref[tile]], out_sems.at[k, q]).start()
        return carry

    lax.fori_loop(0, GROUPS, source, 0)
    for k in range(GROUPS):
        for q in range(per):
            src = held.at[k, pl.ds(q * TILE, TILE)]
            pltpu.make_async_copy(src, out_ref.at[0, 0], out_sems.at[k, q]).wait()


def form(slot, groups, slots, me, pieces, xs, after):
    rows, width = pieces[0].shape[-2:]
    order = xs[0].shape[1]
    count = len(pieces)
    low = jnp.bfloat16
    return pl.pallas_call(
        lambda *refs: form_kernel(slot, count, *refs),
        out_shape=pltpu.HBM((GROUPS, SLOTS, TILE, width), F32),
        in_specs=[smem_spec()] * 3 + [any_spec()] * (count + 2 + len(after)),
        out_specs=any_spec(),
        scratch_shapes=[
            pltpu.VMEM((GROUPS, rows, width), F32),
            pltpu.VMEM((GROUPS, rows, order), low),
            pltpu.VMEM((GROUPS, rows, order), low),
            pltpu.VMEM((width, order), low),
            pltpu.VMEM((width, order), low),
            pltpu.SemaphoreType.DMA((2,)),
            pltpu.SemaphoreType.DMA((2, GROUPS)),
            pltpu.SemaphoreType.DMA((GROUPS,)),
            pltpu.SemaphoreType.DMA((GROUPS, CTILES // GROUPS)),
        ],
        compiler_params=pltpu.CompilerParams(vmem_limit_bytes=32 * 1024 * 1024),
        cost_estimate=pl.CostEstimate(flops=5_000_000_000, transcendentals=0, bytes_accessed=15_000_000),
        name="form",
    )(groups, slots, me, *pieces, *[hbm(x) for x in xs], *after)


def assemble_kernel(rows_ref, cols_ref, *rest):
    parts = rest[: len(CHUNKS)]
    out_ref, acc, sem = rest[len(CHUNKS) :]
    child = pl.program_id(0)

    @pl.when(child == 0)
    def _():
        acc[...] = jnp.zeros_like(acc)

    for s in range(SLOTS):
        row = rows_ref[child, s]
        at = pl.multiple_of(row * TILE, TILE)
        here = slice(s * TILE, (s + 1) * TILE)
        for c, (slot, width) in enumerate(CHUNKS):
            for w in range(width):
                col = cols_ref[child, slot + w]

                @pl.when(jnp.logical_and(row >= 0, col >= 0))
                def _():
                    acc[col, pl.ds(at, TILE), :] += parts[c][0, here, w * TILE : (w + 1) * TILE]

    @pl.when(child == pl.num_programs(0) - 1)
    def _():
        copies = [
            pltpu.make_async_copy(acc.at[b], out_ref.at[:, pl.ds(b * TILE, TILE)], sem.at[b]) for b in range(BLOCK)
        ]
        for copy in copies:
            copy.start()
        for copy in copies:
            copy.wait()


def assemble(rows, cols, parts):
    block = lambda n: pl.BlockSpec((1, WIN, n), lambda c: (c, 0, 0))
    return pl.pallas_call(
        assemble_kernel,
        grid=(GROUPS,),
        out_shape=jax.ShapeDtypeStruct((SIDE, SIDE), F32),
        in_specs=[smem_spec(), smem_spec()] + [block(w * TILE) for _, w in CHUNKS],
        out_specs=any_spec(),
        scratch_shapes=[pltpu.VMEM((BLOCK, SIDE, TILE), F32), pltpu.SemaphoreType.DMA((BLOCK,))],
        compiler_params=pltpu.CompilerParams(vmem_limit_bytes=40 * 1024 * 1024),
        cost_estimate=pl.CostEstimate(flops=0, transcendentals=0, bytes_accessed=40_000_000),
        name="assemble",
    )(rows, cols, *parts)


def local(pivot_block, panel_rows, update_block, tile_map):
    row_me = lax.axis_index("row")
    front_me = lax.axis_index("front")
    col_me = lax.axis_index("col")
    share, order = pivot_block.shape[1:]
    slab = panel_rows[0]

    panel_all = lax.all_gather(slab, "row", axis=0, tiled=True)
    pivot = jnp.broadcast_to(pivot_block[0], (GROUPS, share, order))
    pivot = lax.all_to_all(pivot, "row", split_axis=0, concat_axis=0, tiled=True).reshape(order, order)

    tile_ids = lax.dynamic_index_in_dim(tile_map, front_me * 2 + col_me, 0, keepdims=False)
    starts = window_starts(tile_ids)
    ahead = jnp.take(starts, (row_me + jnp.arange(GROUPS, dtype=jnp.int32)) % GROUPS)
    groups = tile_ids // BLOCK
    slots = jnp.arange(CTILES, dtype=jnp.int32) - jnp.take(starts, groups)
    me = jnp.stack([row_me, ahead[0]])

    ring = lambda k: [(i, (i + k) % GROUPS) for i in range(GROUPS)]
    first, others = pack_columns(starts, ahead, update_block[0])
    first = lax.all_to_all(first, "row", split_axis=0, concat_axis=0, tiled=True)
    arrived = [[first]]
    for sent in others:
        arrived.append([sent[0]] + [lax.ppermute(sent[k], "row", ring(k)) for k in range(1, GROUPS)])

    upper, inverse = factor(pivot, [others[0][0]])
    *xs, own_factor = solve(panel_all, slab, inverse, [first])

    parts = []
    for n, (slot, _) in enumerate(CHUNKS):
        after = arrived[n + 1][1:4] if n + 1 < len(CHUNKS) else []
        sent = form(slot, groups, slots, me, arrived[n], xs, after)
        sent = sent.reshape(GROUPS, WIN, sent.shape[3])
        parts.append(lax.all_to_all(sent, "front", split_axis=0, concat_axis=0, tiled=True))

    child_maps = jnp.take(tile_map, jnp.arange(GROUPS, dtype=jnp.int32) * 2 + col_me, axis=0)
    parent = assemble(slot_targets(child_maps, front_me), slot_targets(child_maps, row_me), parts)
    lower_rows = lax.dynamic_slice_in_dim(upper, row_me * share, share, 1).T
    return (lower_rows[None], own_factor[None], parent[None])


def solution(mesh):
    return jax.shard_map(
        local,
        mesh=mesh,
        in_specs=(
            P(("front", "col"), "row", None),
            P(("front", "col"), "row", None),
            P(("front", "col"), "row", None),
            P(),
        ),
        out_specs=(
            P(("front", "col"), "row", None),
            P(("front", "col"), "row", None),
            P("col", "front", "row"),
        ),
        check_vma=False,
    )
```

```python
import jax
import jax.numpy as jnp
from jax import lax
from jax.experimental import pallas as pl
from jax.experimental.pallas import tpu as pltpu
from jax.sharding import PartitionSpec as P

TILE = 128
BLOCK = 12
SLOTS = 5
GROUPS = 8
CTILES = 32
WIN = SLOTS * TILE
SIDE = BLOCK * TILE
CHUNKS = ((0, 1), (1, 1), (2, 1), (3, 1), (4, 1))
AHEAD = (3, 3, 3, 3)
ORDER = (4, 2, 6, 1, 7, 3, 5)
HI = lax.Precision.HIGHEST
F32 = jnp.float32


def any_spec():
    return pl.BlockSpec(memory_space=pl.ANY)


def hbm(x):
    return pltpu.with_memory_space_constraint(x, pltpu.HBM)


def smem_spec():
    return pl.BlockSpec(memory_space=pltpu.SMEM)


def vmem_spec():
    return pl.BlockSpec(memory_space=pltpu.VMEM)


def window_starts(tile_ids):
    owners = tile_ids // BLOCK
    blocks = jnp.arange(GROUPS, dtype=jnp.int32)
    starts = jnp.sum((owners[..., None, :] < blocks[:, None]).astype(jnp.int32), axis=-1)
    return jnp.minimum(starts, CTILES - SLOTS)


def slot_targets(child_maps, block_me):
    first = jnp.sum((child_maps // BLOCK < block_me).astype(jnp.int32), axis=1)
    first = jnp.minimum(first, CTILES - SLOTS)
    picks = first[:, None] + jnp.arange(SLOTS, dtype=jnp.int32)[None, :]
    tiles = jnp.take_along_axis(child_maps, picks, axis=1)
    return jnp.where(tiles // BLOCK == block_me, tiles - block_me * BLOCK, -1)


def factor_kernel(a_ref, *refs):
    u_ref, v_ref, work, uw = refs[-4:]
    order = a_ref.shape[0]
    sub = lax.broadcasted_iota(jnp.int32, (8, TILE), 0)
    lane = lax.broadcasted_iota(jnp.int32, (8, TILE), 1)
    work[...] = a_ref[...]
    u_ref[...] = jnp.zeros_like(u_ref)
    v_ref[...] = jnp.zeros_like(v_ref)
    for k in range(order // TILE):
        c0 = k * TILE
        c1 = c0 + TILE
        uw[...] = jnp.zeros_like(uw)

        def panel(p, carry):
            r0 = pl.multiple_of(p * 8, 8)
            shift = (TILE - r0) % TILE
            rows = work[pl.ds(c0 + r0, 8), c0:c1]
            eye = (lane == r0 + sub).astype(F32)
            lhs = pltpu.roll(uw[:, 0:TILE], shift, 1)[:, 0:8]
            upd = lax.dot_general(lhs, uw[...], (((0,), (0,)), ((), ())), precision=HI, preferred_element_type=F32)
            ru = rows - upd[:, 0:TILE]
            rw = eye - upd[:, TILE:]
            diag = pltpu.roll(ru, shift, 1)
            cols = [jnp.broadcast_to(diag[:, j : j + 1], (8, TILE)) for j in range(8)]
            pivots = jnp.zeros((8, TILE), F32)
            for j in range(8):
                d = jnp.broadcast_to(cols[j][j : j + 1, :], (8, TILE))
                pivots = jnp.where(sub == j, d, pivots)
                f = jnp.where(sub > j, cols[j] / d, 0.0)
                ru = ru - f * jnp.broadcast_to(ru[j : j + 1, :], (8, TILE))
                rw = rw - f * jnp.broadcast_to(rw[j : j + 1, :], (8, TILE))
                for m in range(j + 1, 8):
                    cols[m] = cols[m] - f * jnp.broadcast_to(cols[m][j : j + 1, :], (8, TILE))
            scale = lax.rsqrt(pivots)
            uw[pl.ds(r0, 8), 0:TILE] = jnp.where(lane >= r0 + sub, ru * scale, 0.0)
            uw[pl.ds(r0, 8), TILE:] = rw * scale
            return carry

        lax.fori_loop(0, TILE // 8, panel, 0)
        w = uw[:, TILE:]
        u_ref[c0:c1, c0:c1] = uw[:, 0:TILE]
        if c1 < order:
            urow = jnp.dot(w, work[c0:c1, c1:], precision=HI, preferred_element_type=F32)
            u_ref[c0:c1, c1:] = urow
            work[c1:, c1:] = work[c1:, c1:] - lax.dot_general(
                urow, urow, (((0,), (0,)), ((), ())), precision=HI, preferred_element_type=F32
            )
        wt = w.T
        v_ref[c0:c1, c0:c1] = wt
        if k:
            above = jnp.dot(u_ref[0:c0, c0:c1], wt, precision=HI, preferred_element_type=F32)
            v_ref[0:c0, c0:c1] = -jnp.dot(v_ref[0:c0, 0:c0], above, precision=HI, preferred_element_type=F32)


def factor(pivot, after):
    whole = jax.ShapeDtypeStruct(pivot.shape, F32)
    return pl.pallas_call(
        factor_kernel,
        out_shape=(whole, whole),
        in_specs=[vmem_spec()] + [any_spec()] * len(after),
        out_specs=(vmem_spec(), vmem_spec()),
        scratch_shapes=[pltpu.VMEM(pivot.shape, F32), pltpu.VMEM((TILE, 2 * TILE), F32)],
        compiler_params=pltpu.CompilerParams(vmem_limit_bytes=16 * 1024 * 1024),
        cost_estimate=pl.CostEstimate(flops=20_000_000_000, transcendentals=0, bytes_accessed=4_000_000),
        name="factor",
    )(pivot, *after)


def split(x):
    high = x.astype(jnp.bfloat16)
    return high, (x - high.astype(F32)).astype(jnp.bfloat16)


def solve_kernel(all_ref, v_ref, *refs):
    high_ref, low_ref, *rhs = refs[-4:]
    order = v_ref.shape[0]
    step = order // len(rhs)

    @pl.when(pl.program_id(0) == 0)
    def _():
        for n, held in enumerate(rhs):
            depth = (n + 1) * step
            vh, vl = split(v_ref[0:depth, n * step : depth])
            held[0:depth] = vh
            held[depth : 2 * depth] = vl
            held[2 * depth :] = vh

    bh, bl = split(all_ref[...])
    for n, held in enumerate(rhs):
        depth = (n + 1) * step
        lhs = jnp.concatenate([bh[:, 0:depth], bh[:, 0:depth], bl[:, 0:depth]], axis=1)
        x = jnp.dot(lhs, held[...], preferred_element_type=F32)
        here = slice(n * step, depth)
        high_ref[:, here], low_ref[:, here] = split(x)


def solve(panel_all, inverse, after):
    order = inverse.shape[0]
    rows = 1024
    half = order // 2
    block = pl.BlockSpec((rows, order), lambda i: (i, 0))
    return pl.pallas_call(
        solve_kernel,
        grid=(panel_all.shape[0] // rows,),
        out_shape=(pltpu.HBM(panel_all.shape, jnp.bfloat16),) * 2,
        in_specs=[block, pl.BlockSpec(inverse.shape, lambda i: (0, 0))] + [any_spec()] * len(after),
        out_specs=(block, block),
        scratch_shapes=[pltpu.VMEM((3 * half, half), jnp.bfloat16), pltpu.VMEM((3 * order, half), jnp.bfloat16)],
        compiler_params=pltpu.CompilerParams(vmem_limit_bytes=40 * 1024 * 1024),
        cost_estimate=pl.CostEstimate(flops=8_000_000_000, transcendentals=0, bytes_accessed=20_000_000),
        name="solve",
    )(hbm(panel_all), inverse, *after)


def pack_columns_kernel(starts_ref, turned_ref, u_ref, first_ref, *rest):
    outs, (held, in_sems, out_sems) = rest[:-3], rest[-3:]
    bands = in_sems.shape[0]
    rows = u_ref.shape[0] // bands
    loads = []
    for b in range(bands):
        band = pl.ds(b * rows, rows)
        loads.append(pltpu.make_async_copy(u_ref.at[band], held.at[band], in_sems.at[b]))
    for load in loads:
        load.start()
    stores = []
    for b in range(bands):
        band = pl.ds(b * rows, rows)
        loads[b].wait()
        for k in range(GROUPS):
            for c, (slot, width) in enumerate(CHUNKS):
                starts = turned_ref if c else starts_ref
                at = pl.multiple_of((starts[k] + slot) * TILE, TILE)
                src = held.at[band, pl.ds(at, width * TILE)]
                dst = outs[(c - 1) * GROUPS + k].at[band] if c else first_ref.at[k, band]
                store = pltpu.make_async_copy(src, dst, out_sems.at[b, c, k])
                store.start()
                stores.append(store)
    for store in stores:
        store.wait()


def pack_columns(starts, turned_starts, update):
    rows = update.shape[0]
    first, *others = (width * TILE for _, width in CHUNKS)
    pieces = tuple(pltpu.HBM((rows, other), F32) for other in others for _ in range(GROUPS))
    outs = pl.pallas_call(
        pack_columns_kernel,
        out_shape=(pltpu.HBM((GROUPS, rows, first), F32), *pieces),
        in_specs=[smem_spec()] * 2 + [any_spec()],
        out_specs=(any_spec(),) * (1 + len(pieces)),
        scratch_shapes=[
            pltpu.VMEM(update.shape, F32),
            pltpu.SemaphoreType.DMA((4,)),
            pltpu.SemaphoreType.DMA((4, len(CHUNKS), GROUPS)),
        ],
        compiler_params=pltpu.CompilerParams(vmem_limit_bytes=20 * 1024 * 1024),
        cost_estimate=pl.CostEstimate(flops=0, transcendentals=0, bytes_accessed=20_000_000),
        name="pack_columns",
    )(starts, turned_starts, hbm(update))
    return outs[0], [outs[1 + n * GROUPS : 1 + (n + 1) * GROUPS] for n in range(len(others))]


def form_kernel(slot, count, group_ref, slot_ref, me_ref, *rest):
    pieces = rest[:count]
    xh_ref, xl_ref = rest[count : count + 2]
    out_ref, held, xh, xl, ph, plow, pick_sems, x_sems, in_sems, out_sems = rest[-10:]
    rows, width = held.shape[1:]
    per = CTILES // GROUPS
    sel = pl.multiple_of((me_ref[1] + slot) * TILE, TILE)

    def slab_of(k):
        return k if count == 1 else (me_ref[0] + GROUPS - k) % GROUPS

    def x_loads(k):
        band = pl.ds(pl.multiple_of(slab_of(k) * rows, rows), rows)
        return [
            pltpu.make_async_copy(src.at[band], dst.at[k], x_sems.at[n, k])
            for n, (src, dst) in enumerate(((xh_ref, xh), (xl_ref, xl)))
        ]

    picks = [
        pltpu.make_async_copy(src.at[pl.ds(sel, width)], dst, pick_sems.at[n])
        for n, (src, dst) in enumerate(((xh_ref, ph), (xl_ref, plow)))
    ]
    for copy in picks:
        copy.start()
    for k in range(GROUPS):
        for copy in x_loads(k):
            copy.start()
        src = pieces[0].at[k] if count == 1 else pieces[k]
        pltpu.make_async_copy(src, held.at[k], in_sems.at[k]).start()
    for copy in picks:
        copy.wait()
    rhs = jnp.concatenate([ph[...], plow[...], ph[...]], axis=1)

    def source(k, carry):
        for copy in x_loads(k):
            copy.wait()
        lhs = jnp.concatenate([xh[k], xh[k], xl[k]], axis=1)
        prod = lax.dot_general(lhs, rhs, (((1,), (1,)), ((), ())), preferred_element_type=F32)
        src = pieces[0].at[0] if count == 1 else pieces[0]
        pltpu.make_async_copy(src, held.at[k], in_sems.at[k]).wait()
        held[k] -= prod
        for q in range(per):
            tile = slab_of(k) * per + q
            src = held.at[k, pl.ds(q * TILE, TILE)]
            pltpu.make_async_copy(src, out_ref.at[group_ref[tile], slot_ref[tile]], out_sems.at[k, q]).start()
        return carry

    lax.fori_loop(0, GROUPS, source, 0)
    for k in range(GROUPS):
        for q in range(per):
            src = held.at[k, pl.ds(q * TILE, TILE)]
            pltpu.make_async_copy(src, out_ref.at[0, 0], out_sems.at[k, q]).wait()


def form(slot, groups, slots, me, pieces, xs):
    rows, width = pieces[0].shape[-2:]
    order = xs[0].shape[1]
    count = len(pieces)
    low = jnp.bfloat16
    return pl.pallas_call(
        lambda *refs: form_kernel(slot, count, *refs),
        out_shape=pltpu.HBM((GROUPS, SLOTS, TILE, width), F32),
        in_specs=[smem_spec()] * 3 + [any_spec()] * (count + 2),
        out_specs=any_spec(),
        scratch_shapes=[
            pltpu.VMEM((GROUPS, rows, width), F32),
            pltpu.VMEM((GROUPS, rows, order), low),
            pltpu.VMEM((GROUPS, rows, order), low),
            pltpu.VMEM((width, order), low),
            pltpu.VMEM((width, order), low),
            pltpu.SemaphoreType.DMA((2,)),
            pltpu.SemaphoreType.DMA((2, GROUPS)),
            pltpu.SemaphoreType.DMA((GROUPS,)),
            pltpu.SemaphoreType.DMA((GROUPS, CTILES // GROUPS)),
        ],
        compiler_params=pltpu.CompilerParams(vmem_limit_bytes=32 * 1024 * 1024),
        cost_estimate=pl.CostEstimate(flops=5_000_000_000, transcendentals=0, bytes_accessed=15_000_000),
        name="form",
    )(groups, slots, me, *pieces, *[hbm(x) for x in xs])


def assemble_kernel(rows_ref, cols_ref, *rest):
    parts = rest[: len(CHUNKS)]
    out_ref, acc, sem = rest[len(CHUNKS) :]
    child = pl.program_id(0)

    @pl.when(child == 0)
    def _():
        acc[...] = jnp.zeros_like(acc)

    for s in range(SLOTS):
        row = rows_ref[child, s]
        at = pl.multiple_of(row * TILE, TILE)
        here = slice(s * TILE, (s + 1) * TILE)
        for c, (slot, width) in enumerate(CHUNKS):
            for w in range(width):
                col = cols_ref[child, slot + w]

                @pl.when(jnp.logical_and(row >= 0, col >= 0))
                def _():
                    acc[col, pl.ds(at, TILE), :] += parts[c][0, here, w * TILE : (w + 1) * TILE]

    @pl.when(child == pl.num_programs(0) - 1)
    def _():
        copies = [
            pltpu.make_async_copy(acc.at[b], out_ref.at[:, pl.ds(b * TILE, TILE)], sem.at[b]) for b in range(BLOCK)
        ]
        for copy in copies:
            copy.start()
        for copy in copies:
            copy.wait()


def assemble(rows, cols, parts):
    block = lambda n: pl.BlockSpec((1, WIN, n), lambda c: (c, 0, 0))
    return pl.pallas_call(
        assemble_kernel,
        grid=(GROUPS,),
        out_shape=jax.ShapeDtypeStruct((SIDE, SIDE), F32),
        in_specs=[smem_spec(), smem_spec()] + [block(w * TILE) for _, w in CHUNKS],
        out_specs=any_spec(),
        scratch_shapes=[pltpu.VMEM((BLOCK, SIDE, TILE), F32), pltpu.SemaphoreType.DMA((BLOCK,))],
        compiler_params=pltpu.CompilerParams(vmem_limit_bytes=40 * 1024 * 1024),
        cost_estimate=pl.CostEstimate(flops=0, transcendentals=0, bytes_accessed=40_000_000),
        name="assemble",
    )(rows, cols, *parts)


def local(pivot_block, panel_rows, update_block, tile_map):
    row_me = lax.axis_index("row")
    front_me = lax.axis_index("front")
    col_me = lax.axis_index("col")
    share, order = pivot_block.shape[1:]
    slab = panel_rows[0]

    panel_all = lax.all_gather(slab, "row", axis=0, tiled=True)
    pivot = jnp.broadcast_to(pivot_block[0], (GROUPS, share, order))
    pivot = lax.all_to_all(pivot, "row", split_axis=0, concat_axis=0, tiled=True).reshape(order, order)

    tile_ids = lax.dynamic_index_in_dim(tile_map, front_me * 2 + col_me, 0, keepdims=False)
    starts = window_starts(tile_ids)
    ahead = jnp.take(starts, (row_me + jnp.arange(GROUPS, dtype=jnp.int32)) % GROUPS)
    groups = tile_ids // BLOCK
    slots = jnp.arange(CTILES, dtype=jnp.int32) - jnp.take(starts, groups)
    me = jnp.stack([row_me, ahead[0]])

    ring = lambda k: [(i, (i + k) % GROUPS) for i in range(GROUPS)]
    first, others = pack_columns(starts, ahead, update_block[0])
    upper, inverse = factor(pivot, [others[0][0]])
    first = lax.all_to_all(first, "row", split_axis=0, concat_axis=0, tiled=True)
    xs = solve(panel_all, inverse, [first])

    *others[0], first = lax.optimization_barrier((*others[0], first))
    arrived = [[first]]
    for sent in others:
        pieces = [sent[0]] + [None] * (GROUPS - 1)
        for k in ORDER:
            pieces[k] = lax.ppermute(sent[k], "row", ring(k))
        arrived.append(pieces)

    parts = []
    for n, (slot, _) in enumerate(CHUNKS):
        sent = form(slot, groups, slots, me, arrived[n], xs)
        if n == 0:
            late, _ = lax.optimization_barrier((slab, sent))
        sent = sent.reshape(GROUPS, WIN, sent.shape[3])
        if n + 1 < len(CHUNKS):
            sent, *_ = lax.optimization_barrier((sent, *[arrived[n + 1][k] for k in ORDER[: AHEAD[n]]]))
        parts.append(lax.all_to_all(sent, "front", split_axis=0, concat_axis=0, tiled=True))
    own_factor = jnp.dot(late, inverse, precision=HI)

    child_maps = jnp.take(tile_map, jnp.arange(GROUPS, dtype=jnp.int32) * 2 + col_me, axis=0)
    parent = assemble(slot_targets(child_maps, front_me), slot_targets(child_maps, row_me), parts)
    lower_rows = lax.dynamic_slice_in_dim(upper, row_me * share, share, 1).T
    return (lower_rows[None], own_factor[None], parent[None])


def solution(mesh):
    return jax.shard_map(
        local,
        mesh=mesh,
        in_specs=(
            P(("front", "col"), "row", None),
            P(("front", "col"), "row", None),
            P(("front", "col"), "row", None),
            P(),
        ),
        out_specs=(
            P(("front", "col"), "row", None),
            P(("front", "col"), "row", None),
            P("col", "front", "row"),
        ),
        check_vma=False,
    )
```

```python
import jax
import jax.numpy as jnp
from jax import lax
from jax.experimental import pallas as pl
from jax.experimental.pallas import tpu as pltpu
from jax.sharding import PartitionSpec as P

TILE = 128
BLOCK = 12
SLOTS = 5
GROUPS = 8
CTILES = 32
WIN = SLOTS * TILE
SIDE = BLOCK * TILE
CHUNKS = ((0, 1), (1, 1), (2, 1), (3, 1), (4, 1))
AHEAD = (3, 3, 3, 3)
ORDER = (4, 2, 6, 1, 7, 3, 5)
HI = lax.Precision.HIGHEST
F32 = jnp.float32


def any_spec():
    return pl.BlockSpec(memory_space=pl.ANY)


def hbm(x):
    return pltpu.with_memory_space_constraint(x, pltpu.HBM)


def smem_spec():
    return pl.BlockSpec(memory_space=pltpu.SMEM)


def vmem_spec():
    return pl.BlockSpec(memory_space=pltpu.VMEM)


def window_starts(tile_ids):
    owners = tile_ids // BLOCK
    blocks = jnp.arange(GROUPS, dtype=jnp.int32)
    starts = jnp.sum((owners[..., None, :] < blocks[:, None]).astype(jnp.int32), axis=-1)
    return jnp.minimum(starts, CTILES - SLOTS)


def slot_targets(child_maps, block_me):
    first = jnp.sum((child_maps // BLOCK < block_me).astype(jnp.int32), axis=1)
    first = jnp.minimum(first, CTILES - SLOTS)
    picks = first[:, None] + jnp.arange(SLOTS, dtype=jnp.int32)[None, :]
    tiles = jnp.take_along_axis(child_maps, picks, axis=1)
    return jnp.where(tiles // BLOCK == block_me, tiles - block_me * BLOCK, -1)


def factor_kernel(a_ref, *refs):
    u_ref, v_ref, work, uw = refs[-4:]
    order = a_ref.shape[0]
    sub = lax.broadcasted_iota(jnp.int32, (8, TILE), 0)
    lane = lax.broadcasted_iota(jnp.int32, (8, TILE), 1)
    work[...] = a_ref[...]
    u_ref[...] = jnp.zeros_like(u_ref)
    v_ref[...] = jnp.zeros_like(v_ref)
    for k in range(order // TILE):
        c0 = k * TILE
        c1 = c0 + TILE
        uw[...] = jnp.zeros_like(uw)

        def panel(p, carry):
            r0 = pl.multiple_of(p * 8, 8)
            shift = (TILE - r0) % TILE
            rows = work[pl.ds(c0 + r0, 8), c0:c1]
            eye = (lane == r0 + sub).astype(F32)
            lhs = pltpu.roll(uw[:, 0:TILE], shift, 1)[:, 0:8]
            upd = lax.dot_general(lhs, uw[...], (((0,), (0,)), ((), ())), precision=HI, preferred_element_type=F32)
            ru = rows - upd[:, 0:TILE]
            rw = eye - upd[:, TILE:]
            diag = pltpu.roll(ru, shift, 1)
            cols = [jnp.broadcast_to(diag[:, j : j + 1], (8, TILE)) for j in range(8)]
            pivots = jnp.zeros((8, TILE), F32)
            for j in range(8):
                d = jnp.broadcast_to(cols[j][j : j + 1, :], (8, TILE))
                pivots = jnp.where(sub == j, d, pivots)
                f = jnp.where(sub > j, cols[j] / d, 0.0)
                ru = ru - f * jnp.broadcast_to(ru[j : j + 1, :], (8, TILE))
                rw = rw - f * jnp.broadcast_to(rw[j : j + 1, :], (8, TILE))
                for m in range(j + 1, 8):
                    cols[m] = cols[m] - f * jnp.broadcast_to(cols[m][j : j + 1, :], (8, TILE))
            scale = lax.rsqrt(pivots)
            uw[pl.ds(r0, 8), 0:TILE] = jnp.where(lane >= r0 + sub, ru * scale, 0.0)
            uw[pl.ds(r0, 8), TILE:] = rw * scale
            return carry

        lax.fori_loop(0, TILE // 8, panel, 0)
        w = uw[:, TILE:]
        u_ref[c0:c1, c0:c1] = uw[:, 0:TILE]
        if c1 < order:
            urow = jnp.dot(w, work[c0:c1, c1:], precision=HI, preferred_element_type=F32)
            u_ref[c0:c1, c1:] = urow
            work[c1:, c1:] = work[c1:, c1:] - lax.dot_general(
                urow, urow, (((0,), (0,)), ((), ())), precision=HI, preferred_element_type=F32
            )
        wt = w.T
        v_ref[c0:c1, c0:c1] = wt
        if k:
            above = jnp.dot(u_ref[0:c0, c0:c1], wt, precision=HI, preferred_element_type=F32)
            v_ref[0:c0, c0:c1] = -jnp.dot(v_ref[0:c0, 0:c0], above, precision=HI, preferred_element_type=F32)


def factor(pivot, after):
    whole = jax.ShapeDtypeStruct(pivot.shape, F32)
    return pl.pallas_call(
        factor_kernel,
        out_shape=(whole, whole),
        in_specs=[vmem_spec()] + [any_spec()] * len(after),
        out_specs=(vmem_spec(), vmem_spec()),
        scratch_shapes=[pltpu.VMEM(pivot.shape, F32), pltpu.VMEM((TILE, 2 * TILE), F32)],
        compiler_params=pltpu.CompilerParams(vmem_limit_bytes=16 * 1024 * 1024),
        cost_estimate=pl.CostEstimate(flops=20_000_000_000, transcendentals=0, bytes_accessed=4_000_000),
        name="factor",
    )(pivot, *after)


def split(x):
    high = x.astype(jnp.bfloat16)
    return high, (x - high.astype(F32)).astype(jnp.bfloat16)


def solve_kernel(all_ref, v_ref, *refs):
    high_ref, low_ref, *rhs = refs[-4:]
    order = v_ref.shape[0]
    step = order // len(rhs)

    @pl.when(pl.program_id(0) == 0)
    def _():
        for n, held in enumerate(rhs):
            depth = (n + 1) * step
            vh, vl = split(v_ref[0:depth, n * step : depth])
            held[0] = vh
            held[1] = vl

    bh, bl = split(all_ref[...])
    for n, held in enumerate(rhs):
        depth = (n + 1) * step
        x = jnp.dot(bh[:, 0:depth], held[0], preferred_element_type=F32)
        x = x + jnp.dot(bh[:, 0:depth], held[1], preferred_element_type=F32)
        x = x + jnp.dot(bl[:, 0:depth], held[0], preferred_element_type=F32)
        here = slice(n * step, depth)
        high_ref[:, here], low_ref[:, here] = split(x)


def solve(panel_all, inverse, after):
    order = inverse.shape[0]
    rows = 1024
    half = order // 2
    block = pl.BlockSpec((rows, order), lambda i: (i, 0))
    return pl.pallas_call(
        solve_kernel,
        grid=(panel_all.shape[0] // rows,),
        out_shape=(pltpu.HBM(panel_all.shape, jnp.bfloat16),) * 2,
        in_specs=[block, pl.BlockSpec(inverse.shape, lambda i: (0, 0))] + [any_spec()] * len(after),
        out_specs=(block, block),
        scratch_shapes=[pltpu.VMEM((2, half, half), jnp.bfloat16), pltpu.VMEM((2, order, half), jnp.bfloat16)],
        compiler_params=pltpu.CompilerParams(vmem_limit_bytes=40 * 1024 * 1024),
        cost_estimate=pl.CostEstimate(flops=8_000_000_000, transcendentals=0, bytes_accessed=20_000_000),
        name="solve",
    )(hbm(panel_all), inverse, *after)


def pack_columns_kernel(starts_ref, turned_ref, u_ref, first_ref, *rest):
    outs, (held, in_sems, out_sems) = rest[:-3], rest[-3:]
    bands = in_sems.shape[0]
    rows = u_ref.shape[0] // bands
    loads = []
    for b in range(bands):
        band = pl.ds(b * rows, rows)
        loads.append(pltpu.make_async_copy(u_ref.at[band], held.at[band], in_sems.at[b]))
    for load in loads:
        load.start()
    stores = []
    for b in range(bands):
        band = pl.ds(b * rows, rows)
        loads[b].wait()
        for k in range(GROUPS):
            for c, (slot, width) in enumerate(CHUNKS):
                starts = turned_ref if c else starts_ref
                at = pl.multiple_of((starts[k] + slot) * TILE, TILE)
                src = held.at[band, pl.ds(at, width * TILE)]
                dst = outs[(c - 1) * GROUPS + k].at[band] if c else first_ref.at[k, band]
                store = pltpu.make_async_copy(src, dst, out_sems.at[b, c, k])
                store.start()
                stores.append(store)
    for store in stores:
        store.wait()


def pack_columns(starts, turned_starts, update):
    rows = update.shape[0]
    first, *others = (width * TILE for _, width in CHUNKS)
    pieces = tuple(pltpu.HBM((rows, other), F32) for other in others for _ in range(GROUPS))
    outs = pl.pallas_call(
        pack_columns_kernel,
        out_shape=(pltpu.HBM((GROUPS, rows, first), F32), *pieces),
        in_specs=[smem_spec()] * 2 + [any_spec()],
        out_specs=(any_spec(),) * (1 + len(pieces)),
        scratch_shapes=[
            pltpu.VMEM(update.shape, F32),
            pltpu.SemaphoreType.DMA((4,)),
            pltpu.SemaphoreType.DMA((4, len(CHUNKS), GROUPS)),
        ],
        compiler_params=pltpu.CompilerParams(vmem_limit_bytes=20 * 1024 * 1024),
        cost_estimate=pl.CostEstimate(flops=0, transcendentals=0, bytes_accessed=20_000_000),
        name="pack_columns",
    )(starts, turned_starts, hbm(update))
    return outs[0], [outs[1 + n * GROUPS : 1 + (n + 1) * GROUPS] for n in range(len(others))]


def form_kernel(slot, count, group_ref, slot_ref, me_ref, *rest):
    pieces = rest[:count]
    xh_ref, xl_ref = rest[count : count + 2]
    out_ref, held, xh, xl, ph, plow, pick_sems, x_sems, in_sems, out_sems = rest[-10:]
    rows, width = held.shape[1:]
    per = CTILES // GROUPS
    sel = pl.multiple_of((me_ref[1] + slot) * TILE, TILE)

    def slab_of(k):
        return k if count == 1 else (me_ref[0] + GROUPS - k) % GROUPS

    def x_loads(k):
        band = pl.ds(pl.multiple_of(slab_of(k) * rows, rows), rows)
        return [
            pltpu.make_async_copy(src.at[band], dst.at[k], x_sems.at[n, k])
            for n, (src, dst) in enumerate(((xh_ref, xh), (xl_ref, xl)))
        ]

    picks = [
        pltpu.make_async_copy(src.at[pl.ds(sel, width)], dst, pick_sems.at[n])
        for n, (src, dst) in enumerate(((xh_ref, ph), (xl_ref, plow)))
    ]
    for copy in picks:
        copy.start()
    for k in range(GROUPS):
        for copy in x_loads(k):
            copy.start()
        src = pieces[0].at[k] if count == 1 else pieces[k]
        pltpu.make_async_copy(src, held.at[k], in_sems.at[k]).start()
    for copy in picks:
        copy.wait()
    rhs = jnp.concatenate([ph[...], plow[...]], axis=0)
    dims = (((1,), (1,)), ((), ()))

    def source(k, carry):
        for copy in x_loads(k):
            copy.wait()
        both = lax.dot_general(xh[k], rhs, dims, preferred_element_type=F32)
        prod = lax.dot_general(xl[k], ph[...], dims, preferred_element_type=F32)
        prod = both[:, 0:width] + both[:, width:] + prod
        src = pieces[0].at[0] if count == 1 else pieces[0]
        pltpu.make_async_copy(src, held.at[k], in_sems.at[k]).wait()
        held[k] -= prod
        for q in range(per):
            tile = slab_of(k) * per + q
            src = held.at[k, pl.ds(q * TILE, TILE)]
            pltpu.make_async_copy(src, out_ref.at[group_ref[tile], slot_ref[tile]], out_sems.at[k, q]).start()
        return carry

    lax.fori_loop(0, GROUPS, source, 0)
    for k in range(GROUPS):
        for q in range(per):
            src = held.at[k, pl.ds(q * TILE, TILE)]
            pltpu.make_async_copy(src, out_ref.at[0, 0], out_sems.at[k, q]).wait()


def form(slot, groups, slots, me, pieces, xs):
    rows, width = pieces[0].shape[-2:]
    order = xs[0].shape[1]
    count = len(pieces)
    low = jnp.bfloat16
    return pl.pallas_call(
        lambda *refs: form_kernel(slot, count, *refs),
        out_shape=pltpu.HBM((GROUPS, SLOTS, TILE, width), F32),
        in_specs=[smem_spec()] * 3 + [any_spec()] * (count + 2),
        out_specs=any_spec(),
        scratch_shapes=[
            pltpu.VMEM((GROUPS, rows, width), F32),
            pltpu.VMEM((GROUPS, rows, order), low),
            pltpu.VMEM((GROUPS, rows, order), low),
            pltpu.VMEM((width, order), low),
            pltpu.VMEM((width, order), low),
            pltpu.SemaphoreType.DMA((2,)),
            pltpu.SemaphoreType.DMA((2, GROUPS)),
            pltpu.SemaphoreType.DMA((GROUPS,)),
            pltpu.SemaphoreType.DMA((GROUPS, CTILES // GROUPS)),
        ],
        compiler_params=pltpu.CompilerParams(vmem_limit_bytes=32 * 1024 * 1024),
        cost_estimate=pl.CostEstimate(flops=5_000_000_000, transcendentals=0, bytes_accessed=15_000_000),
        name="form",
    )(groups, slots, me, *pieces, *[hbm(x) for x in xs])


def add_tiles(rows_ref, cols_ref, child, parts, slots, acc):
    for s in range(SLOTS):
        row = rows_ref[child, s]
        at = pl.multiple_of(row * TILE, TILE)
        here = slice(s * TILE, (s + 1) * TILE)
        for part, slot in zip(parts, slots):
            col = cols_ref[child, slot]

            @pl.when(jnp.logical_and(row >= 0, col >= 0))
            def _():
                acc[col, pl.ds(at, TILE), :] += part[0, here, :]


def collect_kernel(rows_ref, cols_ref, *rest):
    parts, acc = rest[:-1], rest[-1]
    child = pl.program_id(0)

    @pl.when(child == 0)
    def _():
        acc[...] = jnp.zeros_like(acc)

    add_tiles(rows_ref, cols_ref, child, parts, range(len(parts)), acc)


def collect(rows, cols, parts):
    block = pl.BlockSpec((1, WIN, TILE), lambda c: (c, 0, 0))
    shape = (BLOCK, SIDE, TILE)
    return pl.pallas_call(
        collect_kernel,
        grid=(GROUPS,),
        out_shape=jax.ShapeDtypeStruct(shape, F32),
        in_specs=[smem_spec(), smem_spec()] + [block for _ in parts],
        out_specs=vmem_spec(),
        compiler_params=pltpu.CompilerParams(vmem_limit_bytes=24 * 1024 * 1024),
        cost_estimate=pl.CostEstimate(flops=0, transcendentals=0, bytes_accessed=20_000_000),
        name="collect",
    )(rows, cols, *parts)


def finish_kernel(rows_ref, cols_ref, part_ref, acc_ref, out_ref, part, acc, part_sem, in_sems, out_sems):
    def load(b):
        return pltpu.make_async_copy(acc_ref.at[b], acc.at[b], in_sems.at[b])

    def store(b):
        at = pl.multiple_of(b * TILE, TILE)
        return pltpu.make_async_copy(acc.at[b], out_ref.at[:, pl.ds(at, TILE)], out_sems.at[b])

    whole = pltpu.make_async_copy(part_ref, part, part_sem.at[0])
    whole.start()
    for b in range(BLOCK):
        load(b).start()
    whole.wait()

    def column(b, carry):
        load(b).wait()

        def add(child, inner):
            @pl.when(cols_ref[child, SLOTS - 1] == b)
            def _():
                for s in range(SLOTS):
                    row = rows_ref[child, s]

                    @pl.when(row >= 0)
                    def _():
                        at = pl.ds(pl.multiple_of(row * TILE, TILE), TILE)
                        acc[b, at, :] += part[child, s * TILE : (s + 1) * TILE, :]

            return inner

        lax.fori_loop(0, GROUPS, add, 0)
        store(b).start()
        return carry

    lax.fori_loop(0, BLOCK, column, 0)
    for b in range(BLOCK):
        store(b).wait()


def finish(rows, cols, part, acc):
    return pl.pallas_call(
        finish_kernel,
        out_shape=jax.ShapeDtypeStruct((SIDE, SIDE), F32),
        in_specs=[smem_spec(), smem_spec(), any_spec(), any_spec()],
        out_specs=any_spec(),
        scratch_shapes=[
            pltpu.VMEM(part.shape, F32),
            pltpu.VMEM(acc.shape, F32),
            pltpu.SemaphoreType.DMA((1,)),
            pltpu.SemaphoreType.DMA((BLOCK,)),
            pltpu.SemaphoreType.DMA((BLOCK,)),
        ],
        compiler_params=pltpu.CompilerParams(vmem_limit_bytes=24 * 1024 * 1024),
        cost_estimate=pl.CostEstimate(flops=0, transcendentals=0, bytes_accessed=20_000_000),
        name="finish",
    )(rows, cols, part, hbm(acc))


def local(pivot_block, panel_rows, update_block, tile_map):
    row_me = lax.axis_index("row")
    front_me = lax.axis_index("front")
    col_me = lax.axis_index("col")
    share, order = pivot_block.shape[1:]
    slab = panel_rows[0]

    panel_all = lax.all_gather(slab, "row", axis=0, tiled=True)
    pivot = jnp.broadcast_to(pivot_block[0], (GROUPS, share, order))
    pivot = lax.all_to_all(pivot, "row", split_axis=0, concat_axis=0, tiled=True).reshape(order, order)

    tile_ids = lax.dynamic_index_in_dim(tile_map, front_me * 2 + col_me, 0, keepdims=False)
    starts = window_starts(tile_ids)
    ahead = jnp.take(starts, (row_me + jnp.arange(GROUPS, dtype=jnp.int32)) % GROUPS)
    groups = tile_ids // BLOCK
    slots = jnp.arange(CTILES, dtype=jnp.int32) - jnp.take(starts, groups)
    me = jnp.stack([row_me, ahead[0]])

    ring = lambda k: [(i, (i + k) % GROUPS) for i in range(GROUPS)]
    first, others = pack_columns(starts, ahead, update_block[0])
    upper, inverse = factor(pivot, [others[0][0]])
    first = lax.all_to_all(first, "row", split_axis=0, concat_axis=0, tiled=True)
    xs = solve(panel_all, inverse, [first])

    *others[0], first = lax.optimization_barrier((*others[0], first))
    arrived = [[first]]
    for sent in others:
        pieces = [sent[0]] + [None] * (GROUPS - 1)
        for k in ORDER:
            pieces[k] = lax.ppermute(sent[k], "row", ring(k))
        arrived.append(pieces)

    parts = []
    for n, (slot, _) in enumerate(CHUNKS):
        sent = form(slot, groups, slots, me, arrived[n], xs)
        if n == 0:
            late, _ = lax.optimization_barrier((slab, sent))
        sent = sent.reshape(GROUPS, WIN, sent.shape[3])
        if n + 1 < len(CHUNKS):
            sent, *_ = lax.optimization_barrier((sent, *[arrived[n + 1][k] for k in ORDER[: AHEAD[n]]]))
        parts.append(lax.all_to_all(sent, "front", split_axis=0, concat_axis=0, tiled=True))
    own_factor = jnp.dot(late, inverse, precision=HI)

    child_maps = jnp.take(tile_map, jnp.arange(GROUPS, dtype=jnp.int32) * 2 + col_me, axis=0)
    rows, cols = slot_targets(child_maps, front_me), slot_targets(child_maps, row_me)
    parent = finish(rows, cols, parts[-1], collect(rows, cols, parts[:-1]))
    lower_rows = lax.dynamic_slice_in_dim(upper, row_me * share, share, 1).T
    return (lower_rows[None], own_factor[None], parent[None])


def solution(mesh):
    return jax.shard_map(
        local,
        mesh=mesh,
        in_specs=(
            P(("front", "col"), "row", None),
            P(("front", "col"), "row", None),
            P(("front", "col"), "row", None),
            P(),
        ),
        out_specs=(
            P(("front", "col"), "row", None),
            P(("front", "col"), "row", None),
            P("col", "front", "row"),
        ),
        check_vma=False,
    )
```

```python
import jax
import jax.numpy as jnp
from jax import lax
from jax.experimental import pallas as pl
from jax.experimental.pallas import tpu as pltpu
from jax.sharding import PartitionSpec as P

TILE = 128
BLOCK = 12
SLOTS = 5
GROUPS = 8
CTILES = 32
WIN = SLOTS * TILE
SIDE = BLOCK * TILE
CHUNKS = ((0, 1), (1, 1), (2, 1), (3, 1), (4, 1))
AHEAD = (3, 3, 3, 3)
ORDER = (4, 2, 6, 1, 7, 3, 5)
HI = lax.Precision.HIGHEST
F32 = jnp.float32


def any_spec():
    return pl.BlockSpec(memory_space=pl.ANY)


def hbm(x):
    return pltpu.with_memory_space_constraint(x, pltpu.HBM)


def smem_spec():
    return pl.BlockSpec(memory_space=pltpu.SMEM)


def vmem_spec():
    return pl.BlockSpec(memory_space=pltpu.VMEM)


def window_starts(tile_ids):
    owners = tile_ids // BLOCK
    blocks = jnp.arange(GROUPS, dtype=jnp.int32)
    starts = jnp.sum((owners[..., None, :] < blocks[:, None]).astype(jnp.int32), axis=-1)
    return jnp.minimum(starts, CTILES - SLOTS)


def slot_targets(child_maps, block_me):
    first = jnp.sum((child_maps // BLOCK < block_me).astype(jnp.int32), axis=1)
    first = jnp.minimum(first, CTILES - SLOTS)
    picks = first[:, None] + jnp.arange(SLOTS, dtype=jnp.int32)[None, :]
    tiles = jnp.take_along_axis(child_maps, picks, axis=1)
    return jnp.where(tiles // BLOCK == block_me, tiles - block_me * BLOCK, -1)


def factor_kernel(a_ref, *refs):
    u_ref, v_ref, work, uw = refs[-4:]
    order = a_ref.shape[0]
    sub = lax.broadcasted_iota(jnp.int32, (8, TILE), 0)
    lane = lax.broadcasted_iota(jnp.int32, (8, TILE), 1)
    work[...] = a_ref[...]
    u_ref[...] = jnp.zeros_like(u_ref)
    v_ref[...] = jnp.zeros_like(v_ref)
    for k in range(order // TILE):
        c0 = k * TILE
        c1 = c0 + TILE
        uw[...] = jnp.zeros_like(uw)

        def panel(p, carry):
            r0 = pl.multiple_of(p * 8, 8)
            shift = (TILE - r0) % TILE
            rows = work[pl.ds(c0 + r0, 8), c0:c1]
            eye = (lane == r0 + sub).astype(F32)
            lhs = pltpu.roll(uw[:, 0:TILE], shift, 1)[:, 0:8]
            upd = lax.dot_general(lhs, uw[...], (((0,), (0,)), ((), ())), precision=HI, preferred_element_type=F32)
            ru = rows - upd[:, 0:TILE]
            rw = eye - upd[:, TILE:]
            diag = pltpu.roll(ru, shift, 1)
            cols = [jnp.broadcast_to(diag[:, j : j + 1], (8, TILE)) for j in range(8)]
            pivots = jnp.zeros((8, TILE), F32)
            for j in range(8):
                d = jnp.broadcast_to(cols[j][j : j + 1, :], (8, TILE))
                pivots = jnp.where(sub == j, d, pivots)
                f = jnp.where(sub > j, cols[j] / d, 0.0)
                ru = ru - f * jnp.broadcast_to(ru[j : j + 1, :], (8, TILE))
                rw = rw - f * jnp.broadcast_to(rw[j : j + 1, :], (8, TILE))
                for m in range(j + 1, 8):
                    cols[m] = cols[m] - f * jnp.broadcast_to(cols[m][j : j + 1, :], (8, TILE))
            scale = lax.rsqrt(pivots)
            uw[pl.ds(r0, 8), 0:TILE] = jnp.where(lane >= r0 + sub, ru * scale, 0.0)
            uw[pl.ds(r0, 8), TILE:] = rw * scale
            return carry

        lax.fori_loop(0, TILE // 8, panel, 0)
        w = uw[:, TILE:]
        u_ref[c0:c1, c0:c1] = uw[:, 0:TILE]
        if c1 < order:
            urow = jnp.dot(w, work[c0:c1, c1:], precision=HI, preferred_element_type=F32)
            u_ref[c0:c1, c1:] = urow
            work[c1:, c1:] = work[c1:, c1:] - lax.dot_general(
                urow, urow, (((0,), (0,)), ((), ())), precision=HI, preferred_element_type=F32
            )
        wt = w.T
        v_ref[c0:c1, c0:c1] = wt
        if k:
            above = jnp.dot(u_ref[0:c0, c0:c1], wt, precision=HI, preferred_element_type=F32)
            v_ref[0:c0, c0:c1] = -jnp.dot(v_ref[0:c0, 0:c0], above, precision=HI, preferred_element_type=F32)


def factor(pivot, after):
    whole = jax.ShapeDtypeStruct(pivot.shape, F32)
    return pl.pallas_call(
        factor_kernel,
        out_shape=(whole, whole),
        in_specs=[vmem_spec()] + [any_spec()] * len(after),
        out_specs=(vmem_spec(), vmem_spec()),
        scratch_shapes=[pltpu.VMEM(pivot.shape, F32), pltpu.VMEM((TILE, 2 * TILE), F32)],
        compiler_params=pltpu.CompilerParams(vmem_limit_bytes=16 * 1024 * 1024),
        cost_estimate=pl.CostEstimate(flops=20_000_000_000, transcendentals=0, bytes_accessed=4_000_000),
        name="factor",
    )(pivot, *after)


def split(x):
    high = x.astype(jnp.bfloat16)
    return high, (x - high.astype(F32)).astype(jnp.bfloat16)


def solve_kernel(all_ref, v_ref, *refs):
    high_ref, low_ref, *rhs = refs[-4:]
    order = v_ref.shape[0]
    step = order // len(rhs)

    @pl.when(pl.program_id(0) == 0)
    def _():
        for n, held in enumerate(rhs):
            depth = (n + 1) * step
            vh, vl = split(v_ref[0:depth, n * step : depth])
            held[0] = vh
            held[1] = vl

    bh, bl = split(all_ref[...])
    for n, held in enumerate(rhs):
        depth = (n + 1) * step
        x = jnp.dot(bh[:, 0:depth], held[0], preferred_element_type=F32)
        x = x + jnp.dot(bh[:, 0:depth], held[1], preferred_element_type=F32)
        x = x + jnp.dot(bl[:, 0:depth], held[0], preferred_element_type=F32)
        here = slice(n * step, depth)
        high_ref[:, here], low_ref[:, here] = split(x)


def solve(panel_all, inverse, after):
    order = inverse.shape[0]
    rows = 512
    half = order // 2
    block = pl.BlockSpec((rows, order), lambda i: (i, 0))
    return pl.pallas_call(
        solve_kernel,
        grid=(panel_all.shape[0] // rows,),
        out_shape=(pltpu.HBM(panel_all.shape, jnp.bfloat16),) * 2,
        in_specs=[block, pl.BlockSpec(inverse.shape, lambda i: (0, 0))] + [any_spec()] * len(after),
        out_specs=(block, block),
        scratch_shapes=[pltpu.VMEM((2, half, half), jnp.bfloat16), pltpu.VMEM((2, order, half), jnp.bfloat16)],
        compiler_params=pltpu.CompilerParams(vmem_limit_bytes=40 * 1024 * 1024),
        cost_estimate=pl.CostEstimate(flops=8_000_000_000, transcendentals=0, bytes_accessed=20_000_000),
        name="solve",
    )(hbm(panel_all), inverse, *after)


def pack_columns_kernel(starts_ref, turned_ref, u_ref, first_ref, *rest):
    outs, (held, in_sems, out_sems) = rest[:-3], rest[-3:]
    bands = in_sems.shape[0]
    rows = u_ref.shape[0] // bands
    loads = []
    for b in range(bands):
        band = pl.ds(b * rows, rows)
        loads.append(pltpu.make_async_copy(u_ref.at[band], held.at[band], in_sems.at[b]))
    for load in loads:
        load.start()
    stores = []
    for b in range(bands):
        band = pl.ds(b * rows, rows)
        loads[b].wait()
        for k in range(GROUPS):
            for c, (slot, width) in enumerate(CHUNKS):
                starts = turned_ref if c else starts_ref
                at = pl.multiple_of((starts[k] + slot) * TILE, TILE)
                src = held.at[band, pl.ds(at, width * TILE)]
                dst = outs[(c - 1) * GROUPS + k].at[band] if c else first_ref.at[k, band]
                store = pltpu.make_async_copy(src, dst, out_sems.at[b, c, k])
                store.start()
                stores.append(store)
    for store in stores:
        store.wait()


def pack_columns(starts, turned_starts, update):
    rows = update.shape[0]
    first, *others = (width * TILE for _, width in CHUNKS)
    pieces = tuple(pltpu.HBM((rows, other), F32) for other in others for _ in range(GROUPS))
    outs = pl.pallas_call(
        pack_columns_kernel,
        out_shape=(pltpu.HBM((GROUPS, rows, first), F32), *pieces),
        in_specs=[smem_spec()] * 2 + [any_spec()],
        out_specs=(any_spec(),) * (1 + len(pieces)),
        scratch_shapes=[
            pltpu.VMEM(update.shape, F32),
            pltpu.SemaphoreType.DMA((4,)),
            pltpu.SemaphoreType.DMA((4, len(CHUNKS), GROUPS)),
        ],
        compiler_params=pltpu.CompilerParams(vmem_limit_bytes=20 * 1024 * 1024),
        cost_estimate=pl.CostEstimate(flops=0, transcendentals=0, bytes_accessed=20_000_000),
        name="pack_columns",
    )(starts, turned_starts, hbm(update))
    return outs[0], [outs[1 + n * GROUPS : 1 + (n + 1) * GROUPS] for n in range(len(others))]


def form_kernel(slot, count, group_ref, slot_ref, me_ref, *rest):
    pieces = rest[:count]
    xh_ref, xl_ref = rest[count : count + 2]
    out_ref, held, xh, xl, ph, plow, pick_sems, x_sems, in_sems, out_sems = rest[-10:]
    rows, width = held.shape[1:]
    per = CTILES // GROUPS
    sel = pl.multiple_of((me_ref[1] + slot) * TILE, TILE)

    def slab_of(k):
        return k if count == 1 else (me_ref[0] + GROUPS - k) % GROUPS

    def x_loads(k):
        band = pl.ds(pl.multiple_of(slab_of(k) * rows, rows), rows)
        return [
            pltpu.make_async_copy(src.at[band], dst.at[k], x_sems.at[n, k])
            for n, (src, dst) in enumerate(((xh_ref, xh), (xl_ref, xl)))
        ]

    picks = [
        pltpu.make_async_copy(src.at[pl.ds(sel, width)], dst, pick_sems.at[n])
        for n, (src, dst) in enumerate(((xh_ref, ph), (xl_ref, plow)))
    ]
    for copy in picks:
        copy.start()
    for k in range(GROUPS):
        for copy in x_loads(k):
            copy.start()
        src = pieces[0].at[k] if count == 1 else pieces[k]
        pltpu.make_async_copy(src, held.at[k], in_sems.at[k]).start()
    for copy in picks:
        copy.wait()
    rhs = jnp.concatenate([ph[...], plow[...]], axis=0)
    dims = (((1,), (1,)), ((), ()))

    def source(k, carry):
        for copy in x_loads(k):
            copy.wait()
        both = lax.dot_general(xh[k], rhs, dims, preferred_element_type=F32)
        prod = lax.dot_general(xl[k], ph[...], dims, preferred_element_type=F32)
        prod = both[:, 0:width] + both[:, width:] + prod
        src = pieces[0].at[0] if count == 1 else pieces[0]
        pltpu.make_async_copy(src, held.at[k], in_sems.at[k]).wait()
        held[k] -= prod
        for q in range(per):
            tile = slab_of(k) * per + q
            src = held.at[k, pl.ds(q * TILE, TILE)]
            pltpu.make_async_copy(src, out_ref.at[group_ref[tile], slot_ref[tile]], out_sems.at[k, q]).start()
        return carry

    lax.fori_loop(0, GROUPS, source, 0)
    for k in range(GROUPS):
        for q in range(per):
            src = held.at[k, pl.ds(q * TILE, TILE)]
            pltpu.make_async_copy(src, out_ref.at[0, 0], out_sems.at[k, q]).wait()


def form(slot, groups, slots, me, pieces, xs):
    rows, width = pieces[0].shape[-2:]
    order = xs[0].shape[1]
    count = len(pieces)
    low = jnp.bfloat16
    return pl.pallas_call(
        lambda *refs: form_kernel(slot, count, *refs),
        out_shape=pltpu.HBM((GROUPS, SLOTS, TILE, width), F32),
        in_specs=[smem_spec()] * 3 + [any_spec()] * (count + 2),
        out_specs=any_spec(),
        scratch_shapes=[
            pltpu.VMEM((GROUPS, rows, width), F32),
            pltpu.VMEM((GROUPS, rows, order), low),
            pltpu.VMEM((GROUPS, rows, order), low),
            pltpu.VMEM((width, order), low),
            pltpu.VMEM((width, order), low),
            pltpu.SemaphoreType.DMA((2,)),
            pltpu.SemaphoreType.DMA((2, GROUPS)),
            pltpu.SemaphoreType.DMA((GROUPS,)),
            pltpu.SemaphoreType.DMA((GROUPS, CTILES // GROUPS)),
        ],
        compiler_params=pltpu.CompilerParams(vmem_limit_bytes=32 * 1024 * 1024),
        cost_estimate=pl.CostEstimate(flops=5_000_000_000, transcendentals=0, bytes_accessed=15_000_000),
        name="form",
    )(groups, slots, me, *pieces, *[hbm(x) for x in xs])


def add_tiles(rows_ref, cols_ref, child, parts, slots, acc):
    for s in range(SLOTS):
        row = rows_ref[child, s]
        at = pl.multiple_of(row * TILE, TILE)
        here = slice(s * TILE, (s + 1) * TILE)
        for part, slot in zip(parts, slots):
            col = cols_ref[child, slot]

            @pl.when(jnp.logical_and(row >= 0, col >= 0))
            def _():
                acc[col, pl.ds(at, TILE), :] += part[0, here, :]


def collect_kernel(rows_ref, cols_ref, *rest):
    parts, acc = rest[:-1], rest[-1]
    child = pl.program_id(0)

    @pl.when(child == 0)
    def _():
        acc[...] = jnp.zeros_like(acc)

    add_tiles(rows_ref, cols_ref, child, parts, range(len(parts)), acc)


def collect(rows, cols, parts):
    block = pl.BlockSpec((1, WIN, TILE), lambda c: (c, 0, 0))
    shape = (BLOCK, SIDE, TILE)
    return pl.pallas_call(
        collect_kernel,
        grid=(GROUPS,),
        out_shape=jax.ShapeDtypeStruct(shape, F32),
        in_specs=[smem_spec(), smem_spec()] + [block for _ in parts],
        out_specs=vmem_spec(),
        compiler_params=pltpu.CompilerParams(vmem_limit_bytes=24 * 1024 * 1024),
        cost_estimate=pl.CostEstimate(flops=0, transcendentals=0, bytes_accessed=20_000_000),
        name="collect",
    )(rows, cols, *parts)


def finish_kernel(rows_ref, cols_ref, part_ref, acc_ref, out_ref, part, acc, part_sem, in_sems, out_sems):
    def load(b):
        return pltpu.make_async_copy(acc_ref.at[b], acc.at[b], in_sems.at[b])

    def store(b):
        at = pl.multiple_of(b * TILE, TILE)
        return pltpu.make_async_copy(acc.at[b], out_ref.at[:, pl.ds(at, TILE)], out_sems.at[b])

    whole = pltpu.make_async_copy(part_ref, part, part_sem.at[0])
    whole.start()
    for b in range(BLOCK):
        load(b).start()
    whole.wait()

    def column(b, carry):
        load(b).wait()

        def add(child, inner):
            @pl.when(cols_ref[child, SLOTS - 1] == b)
            def _():
                for s in range(SLOTS):
                    row = rows_ref[child, s]

                    @pl.when(row >= 0)
                    def _():
                        at = pl.ds(pl.multiple_of(row * TILE, TILE), TILE)
                        acc[b, at, :] += part[child, s * TILE : (s + 1) * TILE, :]

            return inner

        lax.fori_loop(0, GROUPS, add, 0)
        store(b).start()
        return carry

    lax.fori_loop(0, BLOCK, column, 0)
    for b in range(BLOCK):
        store(b).wait()


def finish(rows, cols, part, acc):
    return pl.pallas_call(
        finish_kernel,
        out_shape=jax.ShapeDtypeStruct((SIDE, SIDE), F32),
        in_specs=[smem_spec(), smem_spec(), any_spec(), any_spec()],
        out_specs=any_spec(),
        scratch_shapes=[
            pltpu.VMEM(part.shape, F32),
            pltpu.VMEM(acc.shape, F32),
            pltpu.SemaphoreType.DMA((1,)),
            pltpu.SemaphoreType.DMA((BLOCK,)),
            pltpu.SemaphoreType.DMA((BLOCK,)),
        ],
        compiler_params=pltpu.CompilerParams(vmem_limit_bytes=24 * 1024 * 1024),
        cost_estimate=pl.CostEstimate(flops=0, transcendentals=0, bytes_accessed=20_000_000),
        name="finish",
    )(rows, cols, part, hbm(acc))


def local(pivot_block, panel_rows, update_block, tile_map):
    row_me = lax.axis_index("row")
    front_me = lax.axis_index("front")
    col_me = lax.axis_index("col")
    share, order = pivot_block.shape[1:]
    slab = panel_rows[0]

    panel_all = lax.all_gather(slab, "row", axis=0, tiled=True)
    pivot = jnp.broadcast_to(pivot_block[0], (GROUPS, share, order))
    pivot = lax.all_to_all(pivot, "row", split_axis=0, concat_axis=0, tiled=True).reshape(order, order)

    tile_ids = lax.dynamic_index_in_dim(tile_map, front_me * 2 + col_me, 0, keepdims=False)
    starts = window_starts(tile_ids)
    ahead = jnp.take(starts, (row_me + jnp.arange(GROUPS, dtype=jnp.int32)) % GROUPS)
    groups = tile_ids // BLOCK
    slots = jnp.arange(CTILES, dtype=jnp.int32) - jnp.take(starts, groups)
    me = jnp.stack([row_me, ahead[0]])

    ring = lambda k: [(i, (i + k) % GROUPS) for i in range(GROUPS)]
    first, others = pack_columns(starts, ahead, update_block[0])
    upper, inverse = factor(pivot, [others[0][0]])
    first = lax.all_to_all(first, "row", split_axis=0, concat_axis=0, tiled=True)
    xs = solve(panel_all, inverse, [first])

    *others[0], first = lax.optimization_barrier((*others[0], first))
    arrived = [[first]]
    for sent in others:
        pieces = [sent[0]] + [None] * (GROUPS - 1)
        for k in ORDER:
            pieces[k] = lax.ppermute(sent[k], "row", ring(k))
        arrived.append(pieces)

    parts = []
    for n, (slot, _) in enumerate(CHUNKS):
        sent = form(slot, groups, slots, me, arrived[n], xs)
        if n == 0:
            late, _ = lax.optimization_barrier((slab, sent))
        sent = sent.reshape(GROUPS, WIN, sent.shape[3])
        if n + 1 < len(CHUNKS):
            sent, *_ = lax.optimization_barrier((sent, *[arrived[n + 1][k] for k in ORDER[: AHEAD[n]]]))
        parts.append(lax.all_to_all(sent, "front", split_axis=0, concat_axis=0, tiled=True))
    own_factor = jnp.dot(late, inverse, precision=HI)

    child_maps = jnp.take(tile_map, jnp.arange(GROUPS, dtype=jnp.int32) * 2 + col_me, axis=0)
    rows, cols = slot_targets(child_maps, front_me), slot_targets(child_maps, row_me)
    parent = finish(rows, cols, parts[-1], collect(rows, cols, parts[:-1]))
    lower_rows = lax.dynamic_slice_in_dim(upper, row_me * share, share, 1).T
    return (lower_rows[None], own_factor[None], parent[None])


def solution(mesh):
    return jax.shard_map(
        local,
        mesh=mesh,
        in_specs=(
            P(("front", "col"), "row", None),
            P(("front", "col"), "row", None),
            P(("front", "col"), "row", None),
            P(),
        ),
        out_specs=(
            P(("front", "col"), "row", None),
            P(("front", "col"), "row", None),
            P("col", "front", "row"),
        ),
        check_vma=False,
    )
```
